512 devices in a mesh: tm: 4 (over y_hi, core), pix: 128 (over x, z, y_lo).
Axes of the slice: x: 4, y: 8 (y_hi: 2, y_lo: 4; y = y_hi * 4 + y_lo), z: 8, core: 2. Of those that a mesh axis runs over, the one named last changes fastest.
Arguments:
- activations: bfloat16 [4, 327680, 256], P('tm', 'pix'), may hold values from -6 to 6
- down_weight: bfloat16 [1024, 256], replicated, may hold values from -0.1875 to 0.1875
- down_bias: float32 [256], replicated, may hold values from -3 to 3
- taps: float32 [9, 256], replicated, may hold values from -2 to 2
- point_weight: bfloat16 [256, 256], replicated, may hold values from -0.375 to 0.375
- time_mix: float32 [4, 4, 256], replicated, may hold values from -3 to 3
- edge_rows: int32 [128, 2, 20], P('pix'), may hold values from 0 to 19, as said below
- cotangent: bfloat16 [4, 81920, 256], P(None, ('pix', 'tm')), may hold values from -6 to 6
Outputs:
- grad_input: bfloat16 [4, 327680, 256], P('tm', 'pix')
- grad_down: float32 [1024, 256], replicated
- grad_bias: float32 [256], replicated
- grad_taps: float32 [9, 256], replicated
- grad_point: float32 [256, 256], replicated
- grad_mix: float32 [4, 4, 256], replicated
The draws below stay inside these ranges and needn't reach their ends.
Inputs may be any that keep to these rules, and one draw needn't show every extreme that they name: Each edge_rows[t, e] is either 0, 1, .., 19 or its reversal; edge_rows[t, 1] equals edge_rows[(t + 1) mod 128, 0].
All inputs are finite; a program needn't handle non-finite values.
Results may differ from the reference program's by a relative error of at most 0.014.
Values may be sent and summed in bfloat16 or wider, within the bound.
No kernel may reach another device: no remote copies, remote signals or barrier semaphores. Data moves between devices by JAX's collectives and lax.ppermute only.
A program may use at most 64 MiB of HBM per device.

```python
import math
import jax
import jax.numpy as jnp
from jax import lax

C = 256
TR = 20
TC = 32
TILES = 128
FRAMES = 4
N8 = 81920
N9 = 327680


def draw_edge_rows(key, part):
    flips = jax.random.randint(key, (TILES,), 0, 2)
    ident = jnp.arange(TR, dtype=jnp.int32)
    backward = TR - 1 - ident
    east_maps = jnp.where(flips[:, None] == 1, backward[None, :], ident[None, :])
    west_maps = jnp.roll(east_maps, 1, axis=0)
    return jnp.stack([west_maps, east_maps], axis=1).astype(jnp.int32)


def block_scale(stream_key, shape, cuts, smallest, top_value):
    def one(dim, blocks):
        draws = jax.random.uniform(jax.random.fold_in(jax.random.fold_in(stream_key, 6), dim), (blocks,), jnp.float32, smallest / len(cuts), top_value / len(cuts))
        return jnp.repeat(jnp.exp(draws), shape[dim] // blocks).reshape((-1,) + (1,) * (len(shape) - dim - 1))

    loudness = one(*cuts[0])
    for cut in cuts[1:]:
        loudness = loudness * one(*cut)
    return loudness


def centred(stream_key, dims, scale, bound, split=(), held_as=jnp.bfloat16):
    gain = block_scale(stream_key, dims, split, -0.22, 0.18) if split else 1.0
    entries = jax.random.normal(stream_key, dims, jnp.float32) * scale * gain
    return jnp.minimum(jnp.maximum(entries, -bound), bound).astype(held_as)


def setup_inputs(seed: int = 0) -> dict:
    seeds = jax.random.split(jax.random.key(seed), 9)
    return {
        "activations": centred(seeds[0], (FRAMES, N9, C), 1.0, 6.0, ((0, 4), (1, 128))),
        "down_weight": centred(seeds[1], (4 * C, C), (4 * C) ** -0.5, 0.1875),
        "down_bias": centred(seeds[2], (C,), 0.5, 3.0, (), jnp.float32),
        "taps": centred(seeds[3], (9, C), 9 ** -0.5, 2.0, (), jnp.float32),
        "point_weight": centred(seeds[4], (C, C), C ** -0.5, 0.375),
        "time_mix": centred(seeds[5], (FRAMES, FRAMES, C), FRAMES ** -0.5, 3.0, (), jnp.float32),
        "edge_rows": draw_edge_rows(jax.random.fold_in(seeds[8], 71), 0),
        "cotangent": centred(seeds[7], (FRAMES, N8, C), 1.0, 6.0, ((1, 512),)),
    }


def depthwise(field, taps, edge_rows):
    west_map = edge_rows[:, 0]
    east_map = edge_rows[:, 1]
    west_col = jnp.roll(field[:, :, :, TC - 1, :], 1, axis=1)
    west_col = jnp.take_along_axis(west_col, jnp.broadcast_to(west_map[None, :, :, None], west_col.shape), axis=2)
    east_col = jnp.roll(field[:, :, :, 0, :], -1, axis=1)
    east_col = jnp.take_along_axis(east_col, jnp.broadcast_to(east_map[None, :, :, None], east_col.shape), axis=2)
    widened = jnp.concatenate([west_col[:, :, :, None, :], field, east_col[:, :, :, None, :]], axis=3)
    widened = jnp.pad(widened, ((0, 0), (0, 0), (1, 1), (0, 0), (0, 0)))
    result = jnp.zeros(field.shape, jnp.float32)
    for row_off in range(3):
        for col_off in range(3):
            result = result + taps[row_off * 3 + col_off] * widened[:, :, row_off:row_off + TR, col_off:col_off + TC, :]
    return result

def reference(activations, down_weight, down_bias, taps, point_weight, time_mix, edge_rows, cotangent):
    total = FRAMES * N8
    rows_in = activations.reshape(total, 4 * C)
    preact = jnp.dot(rows_in, down_weight, preferred_element_type=jnp.float32) + down_bias
    pooled = jax.nn.silu(preact).astype(jnp.bfloat16)
    field = pooled.reshape(FRAMES, TILES, TR, TC, C).astype(jnp.float32)
    spread, pullback = jax.vjp(lambda inner, kern: depthwise(inner, kern, edge_rows), field, taps)
    spread_low = spread.astype(jnp.bfloat16).reshape(total, C)
    mixed_in = (pooled.astype(jnp.float32) + jnp.dot(spread_low, point_weight, preferred_element_type=jnp.float32)).astype(jnp.bfloat16)
    mixed_f = mixed_in.reshape(FRAMES, N8, C).astype(jnp.float32)
    cot_f = cotangent.astype(jnp.float32)
    scale = 1.0 / math.sqrt(FRAMES * N8)
    grad_mix = jnp.einsum('gpc,fpc->fgc', mixed_f, cot_f, precision=lax.Precision.HIGHEST) * scale
    mixed_grad = jnp.einsum('fgc,fpc->gpc', time_mix, cot_f, precision=lax.Precision.HIGHEST).astype(jnp.bfloat16)
    mixed_rows = mixed_grad.reshape(total, C)
    grad_point = jnp.dot(spread_low.T, mixed_rows, preferred_element_type=jnp.float32) * scale
    spread_grad = jnp.dot(mixed_rows, point_weight.T, preferred_element_type=jnp.float32).astype(jnp.bfloat16)
    field_grad, taps_grad = pullback(spread_grad.reshape(FRAMES, TILES, TR, TC, C).astype(jnp.float32))
    pooled_grad = mixed_rows.astype(jnp.float32) + field_grad.reshape(total, C)
    sigma = jax.nn.sigmoid(preact)
    pre_grad = (pooled_grad * (sigma * (1.0 + preact * (1.0 - sigma)))).astype(jnp.bfloat16)
    grad_bias = lax.optimization_barrier(jnp.sum(pre_grad.astype(jnp.float32), axis=0)) * scale
    grad_down = jnp.dot(rows_in.T, pre_grad, preferred_element_type=jnp.float32) * scale
    grad_input = jnp.dot(pre_grad, down_weight.T, preferred_element_type=jnp.float32).astype(jnp.bfloat16)
    return (grad_input.reshape(FRAMES, N9, C), grad_down, grad_bias, taps_grad * scale, grad_point, grad_mix)
```

```python
import math

import jax
import jax.numpy as jnp
from jax import lax
from jax.sharding import Mesh, PartitionSpec as P

C = 256
TR = 20
TC = 32
TM = ("yh", "core")
PIX = ("x", "z", "yl")
RING = ("yh", "yl")
SUM_ROWS = 1306
PAD_ROWS = 1536


def padded_2(cells, sides, width):
    for axis, dim in sides:
        count = lax.axis_size(axis)
        head = lax.slice_in_dim(cells, 0, width, axis=dim)
        tail = lax.slice_in_dim(cells, cells.shape[dim] - width, cells.shape[dim], axis=dim)
        cells = jnp.concatenate(
            [
                lax.ppermute(tail, axis, [(i, (i + 1) % count) for i in range(count)]),
                cells,
                lax.ppermute(head, axis, [((i + 1) % count, i) for i in range(count)]),
            ],
            axis=dim,
        )
    return cells


def scatter_sum(rows, axis):
    count = lax.axis_size(axis)
    low = rows.astype(jnp.bfloat16).reshape(count, rows.shape[0] // count, C)
    got = lax.all_to_all(low, axis, split_axis=0, concat_axis=0, tiled=True)
    return jnp.sum(got.astype(jnp.float32), axis=0)


def copies(rows, axis):
    count = lax.axis_size(axis)
    wide = jnp.broadcast_to(rows[None], (count,) + rows.shape)
    return lax.all_to_all(wide, axis, split_axis=0, concat_axis=0, tiled=True)


def sum_over_devices(parts):
    half = PAD_ROWS // 2
    core = lax.axis_index("core")
    keep = lax.dynamic_slice_in_dim(parts, core * half, half, axis=0)
    send = lax.dynamic_slice_in_dim(parts, (1 - core) * half, half, axis=0)
    got = lax.ppermute(send.astype(jnp.bfloat16), "core", [(0, 1), (1, 0)])
    rows = keep + got.astype(jnp.float32)
    rows = scatter_sum(rows, "x")
    rows = scatter_sum(rows, "z")
    rows = jnp.sum(copies(rows.astype(jnp.bfloat16), RING).astype(jnp.float32), axis=0)
    rows = rows.astype(jnp.bfloat16)
    rows = copies(rows, "z").reshape(-1, C)
    rows = copies(rows, "x").reshape(-1, C)
    rows = lax.all_gather(rows, "core", axis=0, tiled=True)
    return rows.astype(jnp.float32)


def on_device(
    activations, down_weight, down_bias, taps, point_weight, time_mix, edge_rows, cotangent
):
    frames = lax.axis_size(TM)
    tiles = lax.axis_size(PIX)
    pixels = TR * TC
    scale = 1.0 / math.sqrt(frames * tiles * pixels)
    rows_in = activations.reshape(pixels, 4 * C)
    preact = jnp.dot(rows_in, down_weight, preferred_element_type=jnp.float32) + down_bias
    pooled = jax.nn.silu(preact).astype(jnp.bfloat16)
    tile_grid = pooled.reshape(1, TR, TC, C)
    padded = padded_2(tile_grid, ((PIX, 2),), 1)
    west_map = edge_rows[0, 0]
    east_map = edge_rows[0, 1]
    west_col = jnp.take(padded[0, :, 0, :], west_map, axis=0)
    east_col = jnp.take(padded[0, :, TC + 1, :], east_map, axis=0)
    widened = jnp.concatenate([west_col[:, None, :], tile_grid[0], east_col[:, None, :]], axis=1)
    widened = jnp.pad(widened, ((1, 1), (0, 0), (0, 0)))
    spread = jnp.zeros((TR, TC, C), jnp.float32)
    for row_off in range(3):
        for col_off in range(3):
            spread = (
                spread
                + taps[row_off * 3 + col_off]
                * widened[row_off : row_off + TR, col_off : col_off + TC, :]
            )
    spread_low = spread.astype(jnp.bfloat16).reshape(pixels, C)
    mixed_in = (
        pooled.astype(jnp.float32)
        + jnp.dot(spread_low, point_weight, preferred_element_type=jnp.float32)
    ).astype(jnp.bfloat16)
    by_pixel = lax.all_to_all(
        mixed_in.reshape(1, pixels, C), TM, split_axis=1, concat_axis=0, tiled=True
    )
    mix_part = jnp.einsum("gpc,fpc->fgc", by_pixel, cotangent, preferred_element_type=jnp.float32)
    cot_f = cotangent.astype(jnp.float32)
    mixed_acc = jnp.zeros((frames, cotangent.shape[1], C), jnp.float32)
    for source in range(frames):
        mixed_acc = mixed_acc + time_mix[source][:, None, :] * cot_f[source][None, :, :]
    mixed_grad = mixed_acc.astype(jnp.bfloat16)
    back_grad = lax.all_to_all(mixed_grad, TM, split_axis=0, concat_axis=1, tiled=True)
    mixed_rows = back_grad.reshape(pixels, C)
    point_part = jnp.dot(spread_low.T, mixed_rows, preferred_element_type=jnp.float32)
    spread_grad = jnp.dot(mixed_rows, point_weight.T, preferred_element_type=jnp.float32).astype(
        jnp.bfloat16
    )
    grad_float = spread_grad.reshape(TR, TC, C).astype(jnp.float32)
    taps_rows = []
    for row_off in range(3):
        for col_off in range(3):
            taps_rows.append(
                jnp.sum(
                    grad_float * widened[row_off : row_off + TR, col_off : col_off + TC, :],
                    axis=(0, 1),
                )
            )
    taps_part = jnp.stack(taps_rows, axis=0)
    grad_padded = jnp.pad(grad_float, ((2, 2), (2, 2), (0, 0)))
    wide_grad = jnp.zeros((TR + 2, TC + 2, C), jnp.float32)
    for row_off in range(3):
        for col_off in range(3):
            wide_grad = (
                wide_grad
                + taps[row_off * 3 + col_off]
                * grad_padded[2 - row_off : 4 - row_off + TR, 2 - col_off : 4 - col_off + TC, :]
            )
    west_back = jnp.take(wide_grad[1 : TR + 1, 0, :], west_map, axis=0)
    east_back = jnp.take(wide_grad[1 : TR + 1, TC + 1, :], east_map, axis=0)
    outgoing = jnp.stack([west_back, east_back], axis=1)
    incoming = padded_2(outgoing.astype(jnp.bfloat16), ((PIX, 1),), 1).astype(outgoing.dtype)
    inner_grad = wide_grad[1 : TR + 1, 1 : TC + 1, :]
    inner_grad = inner_grad.at[:, 0, :].add(incoming[:, 0, :])
    inner_grad = inner_grad.at[:, TC - 1, :].add(incoming[:, 3, :])
    pooled_grad = mixed_rows.astype(jnp.float32) + inner_grad.reshape(pixels, C)
    sigma = jax.nn.sigmoid(preact)
    pre_grad = (pooled_grad * (sigma * (1.0 + preact * (1.0 - sigma)))).astype(jnp.bfloat16)
    bias_part = jnp.sum(pre_grad.astype(jnp.float32), axis=0)
    down_part = jnp.dot(rows_in.T, pre_grad, preferred_element_type=jnp.float32)
    grad_input = jnp.dot(pre_grad, down_weight.T, preferred_element_type=jnp.float32).astype(
        jnp.bfloat16
    )
    parts = jnp.concatenate(
        [
            down_part,
            point_part,
            mix_part.reshape(frames * frames, C),
            taps_part,
            bias_part.reshape(1, C),
            jnp.zeros((PAD_ROWS - SUM_ROWS, C), jnp.float32),
        ],
        axis=0,
    )
    total = sum_over_devices(parts) * scale
    grad_down = total[:1024]
    grad_point = total[1024:1280]
    grad_mix = total[1280:1296].reshape(frames, frames, C)
    grad_taps = total[1296:1305]
    grad_bias = total[1305]
    return (
        grad_input.reshape(1, 4 * pixels, C),
        grad_down,
        grad_bias,
        grad_taps,
        grad_point,
        grad_mix,
    )


def solution(mesh):
    chips = Mesh(mesh.devices.reshape(2, 2, 4, 8, 4), ("yh", "core", "x", "z", "yl"))
    in_specs = (
        P(TM, PIX, None),
        P(),
        P(),
        P(),
        P(),
        P(),
        P(PIX, None, None),
        P(None, PIX + TM, None),
    )
    out_specs = (P(TM, PIX, None), P(), P(), P(), P(), P())
    return jax.shard_map(
        on_device, mesh=chips, in_specs=in_specs, out_specs=out_specs, check_vma=False
    )
```

```python
import functools
import math

import jax
import jax.numpy as jnp
from jax import lax
from jax.experimental import pallas as pl
from jax.experimental.pallas import tpu as pltpu
from jax.sharding import Mesh, PartitionSpec as P

C = 256
TR = 20
TC = 32
PIXELS = TR * TC
SIDE = 32
TM = ("yh", "core")
PIX = ("x", "z", "yl")
RING = ("yh", "yl")
SUM_ROWS = 1306
PAD_ROWS = 1536
LOW = jnp.bfloat16
F32 = jnp.float32
VMEM_BYTES = 24 << 20


def dot_plain(a, b):
    return jnp.dot(a, b, preferred_element_type=F32)


def dot_rows(a, b):
    return lax.dot_general(a, b, (((1,), (1,)), ((), ())), preferred_element_type=F32)


def every_fourth(ref, first, count):
    return jnp.concatenate([ref[h, pl.ds(first, count, stride=4), :] for h in range(2)], axis=1)


def forward_kernel(act_ref, w_ref, bias_ref, rows_t_ref, pooled_ref, slope_ref, wide_ref):
    for h in range(2):
        wide_ref[h] = act_ref[:, h * 128 : (h + 1) * 128].astype(F32)
    step = PIXELS // 5
    for part in range(5):
        first = part * step
        total = bias_ref[...]
        for child in range(4):
            rows = every_fourth(wide_ref, 4 * first + child, step).astype(LOW)
            total = total + dot_plain(rows, w_ref[child * C : (child + 1) * C, :])
            rows_t_ref[child * C : (child + 1) * C, first : first + step] = rows.T
        sigma = jax.nn.sigmoid(total)
        pooled_ref[first : first + step, :] = (total * sigma).astype(LOW)
        slope_ref[first : first + step, :] = sigma * (1.0 + total * (1.0 - sigma))


def flip_matrix(west_flip, east_flip, yh=None):
    row = lax.broadcasted_iota(jnp.int32, (2 * SIDE, 2 * SIDE), 0)
    col = lax.broadcasted_iota(jnp.int32, (2 * SIDE, 2 * SIDE), 1)
    east = row >= SIDE
    base = jnp.where(east, SIDE, 0)
    local = row - base
    flip = jnp.where(east, east_flip, west_flip)
    local = jnp.where(flip != 0, TR - 1 - local, local)
    if yh is not None:
        place = (local >= 10).astype(jnp.int32)
        rest = local - 10 * place
        other = (rest >= 5).astype(jnp.int32)
        local = jnp.where(place == yh, 0, 16) + 8 * other + rest - 5 * other
    source = base + local
    return (col == source).astype(F32).astype(LOW)


def spread_kernel(
    ids_ref, edge_ref, w_ref, bias_ref, taps_ref, point_ref, pooled_ref,
    wide_low_ref, spread_t_ref, mixed_ref, edge_scr, halo_scr, wide_scr, spread_scr,
):
    edge_scr[...] = jnp.zeros_like(edge_scr)
    for side in range(2):
        for h in range(2):
            edge_scr[h, 4 * SIDE * side : 4 * SIDE * side + 4 * TR, :] = edge_ref[
                side, :, h * 128 : (h + 1) * 128
            ].astype(F32)
    total = bias_ref[...]
    for child in range(4):
        rows = every_fourth(edge_scr, child, 2 * SIDE).astype(LOW)
        total = total + dot_plain(rows, w_ref[child * C : (child + 1) * C, :])
    halo = (total * jax.nn.sigmoid(total)).astype(LOW)
    halo_scr[...] = dot_plain(flip_matrix(ids_ref[2], ids_ref[3]), halo)
    col = lax.broadcasted_iota(jnp.int32, (TC, C), 0)
    for shift in range(3):
        for row in (0, TR + 1):
            wide_scr[shift, row] = jnp.zeros((TC, C), F32)
            wide_low_ref[shift, row] = jnp.zeros((TC, C), LOW)

    def widen(r, carry):
        x = pooled_ref[pl.ds(pl.multiple_of(r * TC, TC), TC), :].astype(F32)
        left = jnp.where(col == 0, halo_scr[pl.ds(r, 1), :], pltpu.roll(x, 1, 0))
        right = jnp.where(col == TC - 1, halo_scr[pl.ds(SIDE + r, 1), :], pltpu.roll(x, TC - 1, 0))
        for shift, value in enumerate((left, x, right)):
            wide_scr[shift, r + 1] = value
            wide_low_ref[shift, r + 1] = value.astype(LOW)
        return carry

    lax.fori_loop(0, TR, widen, 0)

    def convolve(r, carry):
        acc = jnp.zeros((TC, C), F32)
        for row_off in range(3):
            for col_off in range(3):
                tap = taps_ref[row_off * 3 + col_off : row_off * 3 + col_off + 1, :]
                acc = acc + tap * wide_scr[col_off, r + row_off]
        spread_scr[pl.ds(pl.multiple_of(r * TC, TC), TC), :] = acc.astype(LOW)
        return carry

    lax.fori_loop(0, TR, convolve, 0)
    step = PIXELS // 5
    for part in range(5):
        span = slice(part * step, (part + 1) * step)
        rows = spread_scr[span, :]
        mixed_ref[span, :] = (pooled_ref[span, :].astype(F32) + dot_plain(rows, point_ref[...])).astype(LOW)
        spread_t_ref[:, span] = rows.T


def fold(x):
    return jnp.sum(x.reshape(x.shape[0] // 8, 8, C), axis=0)


def backward_kernel(
    ids_ref, near_ref, far_ref, edge_ref, mix_ref, point_ref, taps_ref, wide_ref, spread_t_ref,
    mixed_ref, slope_ref, rows_t_hbm,
    parts_ref, send_ref, pre_ref, mg_scr, sg_scr, edge_scr, halo_scr, rows_scr, sem,
):
    load = pltpu.make_async_copy(rows_t_hbm, rows_scr, sem)
    load.start()
    yh = ids_ref[0]
    core = ids_ref[1]
    frame = yh * 2 + core
    weights = [mix_ref[f, pl.ds(frame, 1), :] for f in range(4)]

    sums = tuple(jnp.zeros((8, C), F32) for _ in range(4))
    for ref, place in ((near_ref, yh), (far_ref, 1 - yh)):
        for other in range(2):
            def chunk(i, sums, ref=ref, place=place, other=other):
                start = pl.multiple_of(i * 32, 32)
                at = pl.multiple_of(place * 320 + other * 160 + i * 32, 32)
                cots = [ref[other, f, pl.ds(start, 32), :].astype(F32) for f in range(4)]
                total = weights[0] * cots[0]
                for f in range(1, 4):
                    total = total + weights[f] * cots[f]
                mg_scr[pl.ds(at, 32), :] = total.astype(LOW)
                mixed = mixed_ref[pl.ds(at, 32), :].astype(F32)
                return tuple(sums[f] + fold(mixed * cots[f]) for f in range(4))

            sums = lax.fori_loop(0, 5, chunk, sums)

    halo_scr[...] = jnp.zeros_like(halo_scr)
    for side in range(2):
        for other in range(2):
            for far in range(2):
                total = weights[0] * edge_ref[other, far, side, 0].astype(F32)
                for f in range(1, 4):
                    total = total + weights[f] * edge_ref[other, far, side, f].astype(F32)
                place = side * SIDE + far * 16 + other * 8
                halo_scr[place : place + 5, :] = total
    flipped = dot_plain(flip_matrix(ids_ref[2], ids_ref[3], yh), halo_scr[...].astype(LOW)).astype(LOW)
    edge_grad = dot_rows(flipped, point_ref[...]).astype(LOW).astype(F32)
    edge_scr[...] = jnp.zeros_like(edge_scr)
    valid = lax.broadcasted_iota(jnp.int32, (SIDE, C), 0) < TR
    for side in range(2):
        base = side * 48
        edge_scr[base + 8 : base + 8 + SIDE, :] = jnp.where(
            valid, edge_grad[side * SIDE : (side + 1) * SIDE, :], 0.0
        )
    for side in range(2):
        base = side * 48
        flip = ids_ref[2 + side] != 0
        total = jnp.zeros((24, C), F32)
        for row_off in range(3):
            plain = 3 * row_off + (2 if side == 0 else 0)
            turned = 3 * (2 - row_off) + (2 if side == 0 else 0)
            tap = jnp.where(flip, taps_ref[turned : turned + 1, :], taps_ref[plain : plain + 1, :])
            start = base + 9 - row_off
            total = total + tap * edge_scr[start : start + 24, :]
        halo_scr[side * SIDE : side * SIDE + 24, :] = total

    col = lax.broadcasted_iota(jnp.int32, (TC, C), 0)
    for part in range(4):
        grad = dot_rows(mg_scr[part * 160 : (part + 1) * 160, :], point_ref[...])
        sg_scr[1, 1 + 5 * part : 6 + 5 * part] = grad.astype(LOW).astype(F32).reshape(5, TC, C)
    for shift in range(3):
        for row in (0, TR + 1):
            sg_scr[shift, row] = jnp.zeros((TC, C), F32)

    def shift_and_taps(r, sums):
        x = sg_scr[1, r + 1]
        sg_scr[0, r + 1] = jnp.where(col == TC - 1, 0.0, pltpu.roll(x, TC - 1, 0))
        sg_scr[2, r + 1] = jnp.where(col == 0, 0.0, pltpu.roll(x, 1, 0))
        return tuple(
            sums[k] + fold(x * wide_ref[k % 3, r + k // 3].astype(F32)) for k in range(9)
        )

    tap_sums = lax.fori_loop(
        0, TR, shift_and_taps, tuple(jnp.zeros((8, C), F32) for _ in range(9))
    )

    def gradient(r, total):
        acc = jnp.zeros((TC, C), F32)
        for row_off in range(3):
            for col_off in range(3):
                tap = taps_ref[row_off * 3 + col_off : row_off * 3 + col_off + 1, :]
                acc = acc + tap * sg_scr[col_off, r + 2 - row_off]
        acc = acc + jnp.where(col == 0, halo_scr[pl.ds(r, 1), :], 0.0)
        acc = acc + jnp.where(col == TC - 1, halo_scr[pl.ds(SIDE + r, 1), :], 0.0)
        rows = pl.ds(pl.multiple_of(r * TC, TC), TC)
        pre = ((mg_scr[rows, :].astype(F32) + acc) * slope_ref[rows, :]).astype(LOW)
        pre_ref[rows, :] = pre
        return total + fold(pre.astype(F32))

    bias_sum = lax.fori_loop(0, TR, gradient, jnp.zeros((8, C), F32))

    parts_ref[1280:PAD_ROWS, :] = jnp.zeros((PAD_ROWS - 1280, C), F32)
    for f in range(4):
        parts_ref[pl.ds(1280 + 4 * f + frame, 1), :] = jnp.sum(sums[f], axis=0, keepdims=True)
    for k in range(9):
        parts_ref[1296 + k : 1297 + k, :] = jnp.sum(tap_sums[k], axis=0, keepdims=True)
    parts_ref[1305:1306, :] = jnp.sum(bias_sum, axis=0, keepdims=True)
    parts_ref[1024:1280, :] = dot_plain(spread_t_ref[...], mg_scr[...])
    load.wait()
    for part in range(4):
        rows = slice(part * C, (part + 1) * C)
        parts_ref[rows, :] = dot_plain(rows_scr[rows, :], pre_ref[...])
    half = PAD_ROWS // 2
    start = pl.multiple_of((1 - core) * half, half)
    send_ref[...] = parts_ref[pl.ds(start, half), :].astype(LOW)


def input_grad_kernel(pre_ref, w_ref, out_ref, wide_ref):
    step = PIXELS // 5
    for part in range(5):
        first = part * step
        for child in range(4):
            rows = dot_rows(pre_ref[first : first + step, :], w_ref[child * C : (child + 1) * C, :])
            for h in range(2):
                wide_ref[h, pl.ds(4 * first + child, step, stride=4), :] = rows[:, h * 128 : (h + 1) * 128]
    for h in range(2):
        out_ref[0, :, h * 128 : (h + 1) * 128] = wide_ref[h].astype(LOW)


def unpack_kernel(scale, low_ref, down_ref, bias_ref, taps_ref, point_ref, mix_ref):
    down_ref[...] = low_ref[0:1024, :].astype(F32) * scale
    point_ref[...] = low_ref[1024:1280, :].astype(F32) * scale
    tail = low_ref[1280:1312, :].astype(F32) * scale
    for f in range(4):
        mix_ref[f] = tail[4 * f : 4 * f + 4, :]
    taps_ref[...] = tail[16:25, :]
    bias_ref[...] = tail[25:26, :]


def shape(dims, dtype):
    return jax.ShapeDtypeStruct(dims, dtype)


SMEM_SPEC = pl.BlockSpec(memory_space=pltpu.SMEM)
VMEM_SPEC = pl.BlockSpec(memory_space=pltpu.VMEM)
ANY_SPEC = pl.BlockSpec(memory_space=pl.ANY)


def call(kernel, name, specs, outs, scratch=()):
    return pl.pallas_call(
        kernel,
        name=name,
        in_specs=specs,
        out_specs=jax.tree.map(lambda _: VMEM_SPEC, outs),
        out_shape=outs,
        scratch_shapes=list(scratch),
        compiler_params=pltpu.CompilerParams(vmem_limit_bytes=VMEM_BYTES),
    )


def scatter_sum(rows, axis):
    count = lax.axis_size(axis)
    low = rows.astype(LOW).reshape(count, rows.shape[0] // count, C)
    got = lax.all_to_all(low, axis, split_axis=0, concat_axis=0, tiled=True)
    return jnp.sum(got.astype(F32), axis=0)


def copies(rows, axis):
    count = lax.axis_size(axis)
    wide = jnp.broadcast_to(rows[None], (count,) + rows.shape)
    return lax.all_to_all(wide, axis, split_axis=0, concat_axis=0, tiled=True)


def sum_over_devices(parts, send):
    half = PAD_ROWS // 2
    core = lax.axis_index("core")
    keep = lax.dynamic_slice_in_dim(parts, core * half, half, axis=0)
    got = lax.ppermute(send, "core", [(0, 1), (1, 0)])
    rows = keep + got.astype(F32)
    rows = scatter_sum(rows, "x")
    rows = scatter_sum(rows, "z")
    rows = jnp.sum(copies(rows.astype(LOW), RING).astype(F32), axis=0)
    rows = rows.astype(LOW)
    rows = copies(rows, "z").reshape(-1, C)
    rows = copies(rows, "x").reshape(-1, C)
    return lax.all_gather(rows, "core", axis=0, tiled=True)


def on_device(
    activations, down_weight, down_bias, taps, point_weight, time_mix, edge_rows, cotangent
):
    frames = cotangent.shape[0]
    tiles = lax.axis_size(PIX)
    scale = 1.0 / math.sqrt(frames * tiles * PIXELS)
    swap = [(0, 1), (1, 0)]
    far_half = lax.ppermute(cotangent, "yh", swap)

    act_cols = activations.reshape(TR, 4 * TC, C)
    cot_cols = cotangent.reshape(frames, TR // frames, TC, C)

    def edge(act_from, cot_at):
        act = act_cols[:, act_from : act_from + 4, :].reshape(4 * TR, C)
        cot = cot_cols[:, :, cot_at, :].reshape(TR, C)
        return jnp.concatenate([act, cot], axis=0)

    ring = [(i, (i + 1) % tiles) for i in range(tiles)]
    back = [(b, a) for a, b in ring]
    from_west = lax.ppermute(edge(4 * TC - 4, TC - 1), PIX, ring)
    from_east = lax.ppermute(edge(0, 0), PIX, back)
    near = lax.all_gather(cotangent, "core")
    edges = jnp.stack([from_west, from_east])
    edge_act = edges[:, : 4 * TR, :]
    edge_cot = edges[:, 4 * TR :, :].reshape(2, frames, TR // frames, C)
    edge_pair = jnp.stack([edge_cot, lax.ppermute(edge_cot, "yh", swap)])
    ids = jnp.stack(
        [
            lax.axis_index("yh").astype(jnp.int32),
            lax.axis_index("core").astype(jnp.int32),
            edge_rows[0, 0, 0],
            edge_rows[0, 1, 0],
        ]
    )
    bias = down_bias.reshape(1, C)
    rows_t, pooled, slope = call(
        forward_kernel,
        "forward",
        [VMEM_SPEC] * 3,
        (shape((4 * C, PIXELS), LOW), shape((PIXELS, C), LOW), shape((PIXELS, C), F32)),
        [pltpu.VMEM((2, 4 * PIXELS, 128), F32)],
    )(activations.reshape(4 * PIXELS, C), down_weight, bias)
    wide, spread_t, mixed = call(
        spread_kernel,
        "spread",
        [SMEM_SPEC] + [VMEM_SPEC] * 6,
        (shape((3, TR + 2, TC, C), LOW), shape((C, PIXELS), LOW), shape((PIXELS, C), LOW)),
        [
            pltpu.VMEM((2, 8 * SIDE, 128), F32),
            pltpu.VMEM((2 * SIDE, C), F32),
            pltpu.VMEM((3, TR + 2, TC, C), F32),
            pltpu.VMEM((PIXELS, C), LOW),
        ],
    )(ids, edge_act, down_weight, bias, taps, point_weight, pooled)
    far = lax.all_gather(far_half, "core")
    edge_all = lax.all_gather(edge_pair, "core")
    parts, send, pre = call(
        backward_kernel,
        "backward",
        [SMEM_SPEC] + [VMEM_SPEC] * 10 + [ANY_SPEC],
        (shape((PAD_ROWS, C), F32), shape((PAD_ROWS // 2, C), LOW), shape((PIXELS, C), LOW)),
        [
            pltpu.VMEM((PIXELS, C), LOW),
            pltpu.VMEM((3, TR + 2, TC, C), F32),
            pltpu.VMEM((96, C), F32),
            pltpu.VMEM((2 * SIDE, C), F32),
            pltpu.VMEM((4 * C, PIXELS), LOW),
            pltpu.SemaphoreType.DMA(()),
        ],
    )(ids, near, far, edge_all, time_mix, point_weight, taps, wide, spread_t, mixed, slope, rows_t)
    grad_input = call(
        input_grad_kernel,
        "input_grad",
        [VMEM_SPEC] * 2,
        shape((1, 4 * PIXELS, C), LOW),
        [pltpu.VMEM((2, 4 * PIXELS, 128), F32)],
    )(pre, down_weight)
    total = sum_over_devices(parts, send)
    grad_down, grad_bias, grad_taps, grad_point, grad_mix = call(
        functools.partial(unpack_kernel, scale),
        "unpack",
        [VMEM_SPEC],
        (
            shape((4 * C, C), F32),
            shape((1, C), F32),
            shape((9, C), F32),
            shape((C, C), F32),
            shape((frames, frames, C), F32),
        ),
    )(total)
    return grad_input, grad_down, grad_bias.reshape(C), grad_taps, grad_point, grad_mix


def solution(mesh):
    yl = mesh.shape["pix"] // 32 if mesh.shape["pix"] >= 128 else 2
    x, z = (4, 8) if mesh.shape["pix"] >= 128 else (2, 2)
    chips = Mesh(mesh.devices.reshape(2, 2, x, z, yl), ("yh", "core", "x", "z", "yl"))
    in_specs = (
        P(TM, PIX, None),
        P(),
        P(),
        P(),
        P(),
        P(),
        P(PIX, None, None),
        P(None, PIX + TM, None),
    )
    out_specs = (P(TM, PIX, None), P(), P(), P(), P(), P())
    return jax.shard_map(
        on_device, mesh=chips, in_specs=in_specs, out_specs=out_specs, check_vma=False
    )
```

```python
import functools
import math

import jax
import jax.numpy as jnp
from jax import lax
from jax.experimental import pallas as pl
from jax.experimental.pallas import tpu as pltpu
from jax.sharding import Mesh, PartitionSpec as P

C = 256
TR = 20
TC = 32
PIXELS = TR * TC
SIDE = 32
TM = ("yh", "core")
PIX = ("x", "z", "yl")
SUM_ROWS = 1306
PAD_ROWS = 1536
LOW = jnp.bfloat16
F32 = jnp.float32
VMEM_BYTES = 24 << 20


def dot_plain(a, b):
    return jnp.dot(a, b, preferred_element_type=F32)


def dot_rows(a, b):
    return lax.dot_general(a, b, (((1,), (1,)), ((), ())), preferred_element_type=F32)


def every_fourth(ref, first, count):
    return jnp.concatenate([ref[h, pl.ds(first, count, stride=4), :] for h in range(2)], axis=1)


def forward_kernel(
    act_hbm, w_ref, bias_ref, rows_t_ref, pooled_ref, slope_ref, act_scr, wide_ref, sems
):
    step = PIXELS // 5
    loads = []
    for part in range(5):
        rows = pl.ds(4 * part * step, 4 * step)
        loads.append(pltpu.make_async_copy(act_hbm.at[rows, :], act_scr.at[rows, :], sems.at[part]))
        loads[part].start()
    for part in range(5):
        first = part * step
        loads[part].wait()
        span = slice(4 * first, 4 * first + 4 * step)
        for h in range(2):
            wide_ref[h, span, :] = act_scr[span, h * 128 : (h + 1) * 128].astype(F32)
        total = bias_ref[...]
        for child in range(4):
            rows = every_fourth(wide_ref, 4 * first + child, step).astype(LOW)
            total = total + dot_plain(rows, w_ref[child * C : (child + 1) * C, :])
            rows_t_ref[child * C : (child + 1) * C, first : first + step] = rows.T
        sigma = jax.nn.sigmoid(total)
        pooled_ref[first : first + step, :] = (total * sigma).astype(LOW)
        slope_ref[first : first + step, :] = sigma * (1.0 + total * (1.0 - sigma))


def flip_matrix(west_flip, east_flip, yh=None, core=None):
    row = lax.broadcasted_iota(jnp.int32, (2 * SIDE, 2 * SIDE), 0)
    col = lax.broadcasted_iota(jnp.int32, (2 * SIDE, 2 * SIDE), 1)
    east = row >= SIDE
    base = jnp.where(east, SIDE, 0)
    local = row - base
    flip = jnp.where(east, east_flip, west_flip)
    local = jnp.where(flip != 0, TR - 1 - local, local)
    if yh is not None:
        place = (local >= 10).astype(jnp.int32)
        rest = local - 10 * place
        other = (rest >= 5).astype(jnp.int32)
        local = jnp.where(place == yh, 0, 16) + jnp.where(other == core, 0, 8) + rest - 5 * other
    source = base + local
    return (col == source).astype(F32).astype(LOW)


def spread_kernel(
    maps_ref, edge_ref, w_ref, bias_ref, taps_ref, point_ref, pooled_ref,
    wide_low_ref, spread_t_ref, mixed_ref, edge_scr, halo_scr, wide_scr, spread_scr,
):
    edge_scr[...] = jnp.zeros_like(edge_scr)
    for side in range(2):
        for h in range(2):
            edge_scr[h, 4 * SIDE * side : 4 * SIDE * side + 4 * TR, :] = edge_ref[
                side, :, h * 128 : (h + 1) * 128
            ].astype(F32)
    total = bias_ref[...]
    for child in range(4):
        rows = every_fourth(edge_scr, child, 2 * SIDE).astype(LOW)
        total = total + dot_plain(rows, w_ref[child * C : (child + 1) * C, :])
    halo = (total * jax.nn.sigmoid(total)).astype(LOW)
    halo_scr[...] = dot_plain(flip_matrix(maps_ref[0, 0, 0], maps_ref[0, 1, 0]), halo)
    col = lax.broadcasted_iota(jnp.int32, (TC, C), 0)
    for shift in range(3):
        for row in (0, TR + 1):
            wide_scr[shift, row] = jnp.zeros((TC, C), F32)
            wide_low_ref[shift, row] = jnp.zeros((TC, C), LOW)

    def widen(r, carry):
        x = pooled_ref[pl.ds(pl.multiple_of(r * TC, TC), TC), :].astype(F32)
        left = jnp.where(col == 0, halo_scr[pl.ds(r, 1), :], pltpu.roll(x, 1, 0))
        right = jnp.where(col == TC - 1, halo_scr[pl.ds(SIDE + r, 1), :], pltpu.roll(x, TC - 1, 0))
        for shift, value in enumerate((left, x, right)):
            wide_scr[shift, r + 1] = value
            wide_low_ref[shift, r + 1] = value.astype(LOW)
        return carry

    lax.fori_loop(0, TR, widen, 0)

    def convolve(r, carry):
        acc = jnp.zeros((TC, C), F32)
        for row_off in range(3):
            for col_off in range(3):
                tap = taps_ref[row_off * 3 + col_off : row_off * 3 + col_off + 1, :]
                acc = acc + tap * wide_scr[col_off, r + row_off]
        spread_scr[pl.ds(pl.multiple_of(r * TC, TC), TC), :] = acc.astype(LOW)
        return carry

    lax.fori_loop(0, TR, convolve, 0)
    step = PIXELS // 5
    for part in range(5):
        span = slice(part * step, (part + 1) * step)
        rows = spread_scr[span, :]
        mixed_ref[span, :] = (pooled_ref[span, :].astype(F32) + dot_plain(rows, point_ref[...])).astype(LOW)
        spread_t_ref[:, span] = rows.T


def fold(x):
    return jnp.sum(x.reshape(x.shape[0] // 8, 8, C), axis=0)


def backward_kernel(
    maps_ref, own_ref, other_ref, mix_ref, point_ref, taps_ref, wide_ref, spread_t_ref,
    mixed_ref, slope_ref, rows_t_hbm,
    keep_ref, send_ref, pre_ref, mg_scr, sg_scr, edge_scr, halo_scr, rows_scr, sem,
):
    load = pltpu.make_async_copy(rows_t_hbm, rows_scr, sem)
    load.start()
    yh = lax.axis_index("yh")
    core = lax.axis_index("core")
    frame = yh * 2 + core
    weights = [mix_ref[f, pl.ds(frame, 1), :] for f in range(4)]

    sums = tuple(jnp.zeros((8, C), F32) for _ in range(4))
    for ref, owner in ((own_ref, core), (other_ref, 1 - core)):
        for far in range(2):
            place = yh if far == 0 else 1 - yh

            def chunk(i, sums, ref=ref, far=far, base=place * 320 + owner * 160):
                start = pl.multiple_of(i * 32, 32)
                at = pl.multiple_of(base + i * 32, 32)
                cots = [
                    ref[pl.ds(far * 640 + f * 160 + start, 32), :].astype(F32) for f in range(4)
                ]
                total = weights[0] * cots[0]
                for f in range(1, 4):
                    total = total + weights[f] * cots[f]
                mg_scr[pl.ds(at, 32), :] = total.astype(LOW)
                mixed = mixed_ref[pl.ds(at, 32), :].astype(F32)
                return tuple(sums[f] + fold(mixed * cots[f]) for f in range(4))

            sums = lax.fori_loop(0, 5, chunk, sums)

    halo_scr[...] = jnp.zeros_like(halo_scr)
    for index, ref in enumerate((own_ref, other_ref)):
        for far in range(2):
            for side in range(2):
                start = 1280 + far * 64 + side * 32
                group = ref[start : start + 32, :].astype(F32)
                total = weights[0] * group[0:5]
                for f in range(1, 4):
                    total = total + weights[f] * group[8 * f : 8 * f + 5]
                place = side * SIDE + far * 16 + index * 8
                halo_scr[place : place + 5, :] = total
    flipped = dot_plain(flip_matrix(maps_ref[0, 0, 0], maps_ref[0, 1, 0], yh, core), halo_scr[...].astype(LOW)).astype(LOW)
    edge_grad = dot_rows(flipped, point_ref[...]).astype(LOW).astype(F32)
    edge_scr[...] = jnp.zeros_like(edge_scr)
    valid = lax.broadcasted_iota(jnp.int32, (SIDE, C), 0) < TR
    for side in range(2):
        base = side * 48
        edge_scr[base + 8 : base + 8 + SIDE, :] = jnp.where(
            valid, edge_grad[side * SIDE : (side + 1) * SIDE, :], 0.0
        )
    for side in range(2):
        base = side * 48
        flip = maps_ref[0, side, 0] != 0
        total = jnp.zeros((24, C), F32)
        for row_off in range(3):
            plain = 3 * row_off + (2 if side == 0 else 0)
            turned = 3 * (2 - row_off) + (2 if side == 0 else 0)
            tap = jnp.where(flip, taps_ref[turned : turned + 1, :], taps_ref[plain : plain + 1, :])
            start = base + 9 - row_off
            total = total + tap * edge_scr[start : start + 24, :]
        halo_scr[side * SIDE : side * SIDE + 24, :] = total

    col = lax.broadcasted_iota(jnp.int32, (TC, C), 0)
    for part in range(4):
        grad = dot_rows(mg_scr[part * 160 : (part + 1) * 160, :], point_ref[...])
        sg_scr[1, 1 + 5 * part : 6 + 5 * part] = grad.astype(LOW).astype(F32).reshape(5, TC, C)
    for shift in range(3):
        for row in (0, TR + 1):
            sg_scr[shift, row] = jnp.zeros((TC, C), F32)

    def shift_and_taps(r, sums):
        x = sg_scr[1, r + 1]
        sg_scr[0, r + 1] = jnp.where(col == TC - 1, 0.0, pltpu.roll(x, TC - 1, 0))
        sg_scr[2, r + 1] = jnp.where(col == 0, 0.0, pltpu.roll(x, 1, 0))
        return tuple(
            sums[k] + fold(x * wide_ref[k % 3, r + k // 3].astype(F32)) for k in range(9)
        )

    tap_sums = lax.fori_loop(
        0, TR, shift_and_taps, tuple(jnp.zeros((8, C), F32) for _ in range(9))
    )

    def gradient(r, total):
        acc = jnp.zeros((TC, C), F32)
        for row_off in range(3):
            for col_off in range(3):
                tap = taps_ref[row_off * 3 + col_off : row_off * 3 + col_off + 1, :]
                acc = acc + tap * sg_scr[col_off, r + 2 - row_off]
        acc = acc + jnp.where(col == 0, halo_scr[pl.ds(r, 1), :], 0.0)
        acc = acc + jnp.where(col == TC - 1, halo_scr[pl.ds(SIDE + r, 1), :], 0.0)
        rows = pl.ds(pl.multiple_of(r * TC, TC), TC)
        pre = ((mg_scr[rows, :].astype(F32) + acc) * slope_ref[rows, :]).astype(LOW)
        pre_ref[rows, :] = pre
        return total + fold(pre.astype(F32))

    bias_sum = lax.fori_loop(0, TR, gradient, jnp.zeros((8, C), F32))

    half = PAD_ROWS // 2

    def put(first, value):
        rows = slice(first % half, first % half + value.shape[0])
        mine = core == first // half

        @pl.when(mine)
        def _():
            keep_ref[rows, :] = value

        @pl.when(jnp.logical_not(mine))
        def _():
            send_ref[rows, :] = value.astype(LOW)

    tail = lax.broadcasted_iota(jnp.int32, (32, C), 0)
    total = jnp.zeros((32, C), F32)
    for f in range(4):
        total = jnp.where(tail == 4 * f + frame, jnp.sum(sums[f], axis=0, keepdims=True), total)
    for k in range(9):
        total = jnp.where(tail == 16 + k, jnp.sum(tap_sums[k], axis=0, keepdims=True), total)
    total = jnp.where(tail == 25, jnp.sum(bias_sum, axis=0, keepdims=True), total)
    put(1280, total)
    put(1312, jnp.zeros((PAD_ROWS - 1312, C), F32))
    put(1024, dot_plain(spread_t_ref[...], mg_scr[...]))
    load.wait()
    for part in range(4):
        put(part * C, dot_plain(rows_scr[part * C : (part + 1) * C, :], pre_ref[...]))


def input_grad_kernel(pre_ref, w_ref, out_ref, wide_ref):
    step = PIXELS // 5
    for part in range(5):
        first = part * step
        for child in range(4):
            rows = dot_rows(pre_ref[first : first + step, :], w_ref[child * C : (child + 1) * C, :])
            for h in range(2):
                wide_ref[h, pl.ds(4 * first + child, step, stride=4), :] = rows[:, h * 128 : (h + 1) * 128]
    for h in range(2):
        out_ref[0, :, h * 128 : (h + 1) * 128] = wide_ref[h].astype(LOW)


def unpack_kernel(scale, low_ref, down_ref, bias_ref, taps_ref, point_ref, mix_ref):
    down_ref[...] = low_ref[0:1024, :].astype(F32) * scale
    point_ref[...] = low_ref[1024:1280, :].astype(F32) * scale
    tail = low_ref[1280:1312, :].astype(F32) * scale
    for f in range(4):
        mix_ref[f] = tail[4 * f : 4 * f + 4, :]
    taps_ref[...] = tail[16:25, :]
    bias_ref[...] = tail[25:26, :]


def shape(dims, dtype):
    return jax.ShapeDtypeStruct(dims, dtype)


SMEM_SPEC = pl.BlockSpec(memory_space=pltpu.SMEM)
VMEM_SPEC = pl.BlockSpec(memory_space=pltpu.VMEM)
ANY_SPEC = pl.BlockSpec(memory_space=pl.ANY)


def call(kernel, name, specs, outs, scratch=()):
    return pl.pallas_call(
        kernel,
        name=name,
        in_specs=specs,
        out_specs=jax.tree.map(lambda _: VMEM_SPEC, outs),
        out_shape=outs,
        scratch_shapes=list(scratch),
        compiler_params=pltpu.CompilerParams(vmem_limit_bytes=VMEM_BYTES),
    )


def scatter_sum(rows, axis):
    count = lax.axis_size(axis)
    low = rows.astype(LOW).reshape(count, rows.shape[0] // count, C)
    got = lax.all_to_all(low, axis, split_axis=0, concat_axis=0, tiled=True)
    return jnp.sum(got.astype(F32), axis=0)


def copies(rows, axis):
    count = lax.axis_size(axis)
    wide = jnp.broadcast_to(rows[None], (count,) + rows.shape)
    return lax.all_to_all(wide, axis, split_axis=0, concat_axis=0, tiled=True)


def sum_over_devices(keep, send):
    got = lax.ppermute(send, "core", [(0, 1), (1, 0)])
    rows = keep + got.astype(F32)
    rows = scatter_sum(rows, ("x", "z"))
    rows = jnp.sum(copies(rows.astype(LOW), ("yh", "yl")).astype(F32), axis=0)
    rows = copies(rows.astype(LOW), ("x", "z")).reshape(-1, C)
    return lax.all_gather(rows, "core", axis=0, tiled=True)


def on_device(
    activations, down_weight, down_bias, taps, point_weight, time_mix, edge_rows, cotangent
):
    frames = cotangent.shape[0]
    tiles = lax.axis_size(PIX)
    scale = 1.0 / math.sqrt(frames * tiles * PIXELS)
    swap = [(0, 1), (1, 0)]
    far_half = lax.ppermute(cotangent, "yh", swap)

    act_cols = activations.reshape(TR, 4 * TC, C)
    cot_cols = cotangent.reshape(frames, TR // frames, TC, C)
    even = lax.axis_index("yl") % 2 == 0
    west_act = act_cols[:, :4, :].reshape(4 * TR, C)
    east_act = act_cols[:, 4 * TC - 4 :, :].reshape(4 * TR, C)
    west_cot = cot_cols[:, :, 0, :].reshape(TR, C)
    east_cot = cot_cols[:, :, TC - 1, :].reshape(TR, C)

    def exchange(west, east, axes, hops):
        first = lax.ppermute(jnp.where(even, east, west), axes, hops(lambda i: i ^ 1))
        second = lax.ppermute(
            jnp.where(even, west, east), axes, hops(lambda i: (i + 2 * (i % 2) - 1) % tiles)
        )
        return jnp.where(even, second, first), jnp.where(even, first, second)

    from_west, from_east = exchange(
        jnp.concatenate([west_act, west_cot], axis=0),
        jnp.concatenate([east_act, east_cot], axis=0),
        PIX,
        lambda partner: [(i, partner(i)) for i in range(tiles)],
    )
    cross = exchange(
        west_cot,
        east_cot,
        ("yh",) + PIX,
        lambda partner: [
            (y * tiles + i, (1 - y) * tiles + partner(i)) for y in range(2) for i in range(tiles)
        ],
    )
    bias = down_bias.reshape(1, C)
    rows_t, pooled, slope = call(
        forward_kernel,
        "forward",
        [ANY_SPEC] + [VMEM_SPEC] * 2,
        (shape((4 * C, PIXELS), LOW), shape((PIXELS, C), LOW), shape((PIXELS, C), F32)),
        [
            pltpu.VMEM((4 * PIXELS, C), LOW),
            pltpu.VMEM((2, 4 * PIXELS, 128), F32),
            pltpu.SemaphoreType.DMA((5,)),
        ],
    )(activations.reshape(4 * PIXELS, C), down_weight, bias)
    from_west, from_east, cross, pooled = lax.optimization_barrier(
        (from_west, from_east, cross, pooled)
    )
    edge_act = jnp.stack([from_west[: 4 * TR], from_east[: 4 * TR]])
    edge_pair = jnp.pad(
        jnp.stack([from_west[4 * TR :], from_east[4 * TR :], *cross]).reshape(
            4 * frames, TR // frames, C
        ),
        ((0, 0), (0, 3), (0, 0)),
    ).reshape(16 * 8, C)
    own = jnp.concatenate(
        [cotangent.reshape(PIXELS, C), far_half.reshape(PIXELS, C), edge_pair], axis=0
    )
    other = lax.ppermute(own, "core", swap)
    wide, spread_t, mixed = call(
        spread_kernel,
        "spread",
        [SMEM_SPEC] + [VMEM_SPEC] * 6,
        (shape((3, TR + 2, TC, C), LOW), shape((C, PIXELS), LOW), shape((PIXELS, C), LOW)),
        [
            pltpu.VMEM((2, 8 * SIDE, 128), F32),
            pltpu.VMEM((2 * SIDE, C), F32),
            pltpu.VMEM((3, TR + 2, TC, C), F32),
            pltpu.VMEM((PIXELS, C), LOW),
        ],
    )(edge_rows, edge_act, down_weight, bias, taps, point_weight, pooled)
    keep, send, pre = call(
        backward_kernel,
        "backward",
        [SMEM_SPEC] + [VMEM_SPEC] * 9 + [ANY_SPEC],
        (shape((PAD_ROWS // 2, C), F32), shape((PAD_ROWS // 2, C), LOW), shape((PIXELS, C), LOW)),
        [
            pltpu.VMEM((PIXELS, C), LOW),
            pltpu.VMEM((3, TR + 2, TC, C), F32),
            pltpu.VMEM((96, C), F32),
            pltpu.VMEM((2 * SIDE, C), F32),
            pltpu.VMEM((4 * C, PIXELS), LOW),
            pltpu.SemaphoreType.DMA(()),
        ],
    )(edge_rows, own, other, time_mix, point_weight, taps, wide, spread_t, mixed, slope, rows_t)
    grad_input = call(
        input_grad_kernel,
        "input_grad",
        [VMEM_SPEC] * 2,
        shape((1, 4 * PIXELS, C), LOW),
        [pltpu.VMEM((2, 4 * PIXELS, 128), F32)],
    )(pre, down_weight)
    total = sum_over_devices(keep, send)
    grad_down, grad_bias, grad_taps, grad_point, grad_mix = call(
        functools.partial(unpack_kernel, scale),
        "unpack",
        [VMEM_SPEC],
        (
            shape((4 * C, C), F32),
            shape((1, C), F32),
            shape((9, C), F32),
            shape((C, C), F32),
            shape((frames, frames, C), F32),
        ),
    )(total)
    return grad_input, grad_down, grad_bias.reshape(C), grad_taps, grad_point, grad_mix


def solution(mesh):
    yl = mesh.shape["pix"] // 32 if mesh.shape["pix"] >= 128 else 2
    x, z = (4, 8) if mesh.shape["pix"] >= 128 else (2, 2)
    chips = Mesh(mesh.devices.reshape(2, 2, x, z, yl), ("yh", "core", "x", "z", "yl"))
    in_specs = (
        P(TM, PIX, None),
        P(),
        P(),
        P(),
        P(),
        P(),
        P(PIX, None, None),
        P(None, PIX + TM, None),
    )
    out_specs = (P(TM, PIX, None), P(), P(), P(), P(), P())
    return jax.shard_map(
        on_device, mesh=chips, in_specs=in_specs, out_specs=out_specs, check_vma=False
    )
```

```python
import functools
import math

import jax
import jax.numpy as jnp
from jax import lax
from jax.experimental import pallas as pl
from jax.experimental.pallas import tpu as pltpu
from jax.sharding import Mesh, PartitionSpec as P

C = 256
TR = 20
TC = 32
PIXELS = TR * TC
SIDE = 32
TM = ("yh", "core")
PIX = ("x", "z", "yl")
SUM_ROWS = 1306
PAD_ROWS = 1536
LOW = jnp.bfloat16
F32 = jnp.float32
VMEM_BYTES = 24 << 20


def dot_plain(a, b):
    return jnp.dot(a, b, preferred_element_type=F32)


def dot_rows(a, b):
    return lax.dot_general(a, b, (((1,), (1,)), ((), ())), preferred_element_type=F32)


def every_fourth(ref, first, count):
    return jnp.concatenate([ref[h, pl.ds(first, count, stride=4), :] for h in range(2)], axis=1)


def forward_kernel(act_ref, w_ref, bias_ref, rows_t_ref, pooled_ref, slope_ref, wide_ref):
    step = PIXELS // 5
    for part in range(5):
        first = part * step
        span = slice(4 * first, 4 * first + 4 * step)
        for h in range(2):
            wide_ref[h, span, :] = act_ref[span, h * 128 : (h + 1) * 128].astype(F32)
        total = bias_ref[...]
        for child in range(4):
            rows = every_fourth(wide_ref, 4 * first + child, step).astype(LOW)
            total = total + dot_plain(rows, w_ref[child * C : (child + 1) * C, :])
            rows_t_ref[child * C : (child + 1) * C, first : first + step] = rows.T
        sigma = jax.nn.sigmoid(total)
        pooled_ref[first : first + step, :] = (total * sigma).astype(LOW)
        slope_ref[first : first + step, :] = sigma * (1.0 + total * (1.0 - sigma))


def flip_matrix(west_flip, east_flip, yh=None, core=None):
    row = lax.broadcasted_iota(jnp.int32, (2 * SIDE, 2 * SIDE), 0)
    col = lax.broadcasted_iota(jnp.int32, (2 * SIDE, 2 * SIDE), 1)
    east = row >= SIDE
    base = jnp.where(east, SIDE, 0)
    local = row - base
    flip = jnp.where(east, east_flip, west_flip)
    local = jnp.where(flip != 0, TR - 1 - local, local)
    if yh is not None:
        place = (local >= 10).astype(jnp.int32)
        rest = local - 10 * place
        other = (rest >= 5).astype(jnp.int32)
        local = jnp.where(place == yh, 0, 16) + jnp.where(other == core, 0, 8) + rest - 5 * other
    source = base + local
    return (col == source).astype(F32).astype(LOW)


def spread_kernel(
    maps_ref, edge_ref, w_ref, bias_ref, taps_ref, point_ref, pooled_ref,
    wide_low_ref, spread_t_ref, mixed_ref, edge_scr, halo_scr, wide_scr, spread_scr,
):
    edge_scr[...] = jnp.zeros_like(edge_scr)
    for side in range(2):
        for h in range(2):
            edge_scr[h, 4 * SIDE * side : 4 * SIDE * side + 4 * TR, :] = edge_ref[
                side, :, h * 128 : (h + 1) * 128
            ].astype(F32)
    total = bias_ref[...]
    for child in range(4):
        rows = every_fourth(edge_scr, child, 2 * SIDE).astype(LOW)
        total = total + dot_plain(rows, w_ref[child * C : (child + 1) * C, :])
    halo = (total * jax.nn.sigmoid(total)).astype(LOW)
    halo_scr[...] = dot_plain(flip_matrix(maps_ref[0, 0, 0], maps_ref[0, 1, 0]), halo)
    col = lax.broadcasted_iota(jnp.int32, (TC, C), 0)
    for shift in range(3):
        for row in (0, TR + 1):
            wide_scr[shift, row] = jnp.zeros((TC, C), F32)
            wide_low_ref[shift, row] = jnp.zeros((TC, C), LOW)

    def widen(step, carry):
        for r in (2 * step, 2 * step + 1):
            widen_row(r)
        return carry

    def widen_row(r):
        x = pooled_ref[pl.ds(pl.multiple_of(r * TC, TC), TC), :].astype(F32)
        left = jnp.where(col == 0, halo_scr[pl.ds(r, 1), :], pltpu.roll(x, 1, 0))
        right = jnp.where(col == TC - 1, halo_scr[pl.ds(SIDE + r, 1), :], pltpu.roll(x, TC - 1, 0))
        for shift, value in enumerate((left, x, right)):
            wide_scr[shift, r + 1] = value
            wide_low_ref[shift, r + 1] = value.astype(LOW)

    lax.fori_loop(0, TR // 2, widen, 0)

    def convolve(step, carry):
        for r in (2 * step, 2 * step + 1):
            convolve_row(r)
        return carry

    def convolve_row(r):
        acc = jnp.zeros((TC, C), F32)
        for row_off in range(3):
            for col_off in range(3):
                tap = taps_ref[row_off * 3 + col_off : row_off * 3 + col_off + 1, :]
                acc = acc + tap * wide_scr[col_off, r + row_off]
        spread_scr[pl.ds(pl.multiple_of(r * TC, TC), TC), :] = acc.astype(LOW)

    lax.fori_loop(0, TR // 2, convolve, 0)
    step = PIXELS // 5
    for part in range(5):
        span = slice(part * step, (part + 1) * step)
        rows = spread_scr[span, :]
        mixed_ref[span, :] = (pooled_ref[span, :].astype(F32) + dot_plain(rows, point_ref[...])).astype(LOW)
        spread_t_ref[:, span] = rows.T


def fold(x):
    return jnp.sum(x.reshape(x.shape[0] // 8, 8, C), axis=0)


def backward_kernel(
    maps_ref, own_ref, other_ref, mix_ref, point_ref, taps_ref, wide_ref, spread_t_ref,
    mixed_ref, slope_ref, rows_t_ref,
    keep_ref, send_ref, pre_ref, mg_scr, sg_scr, edge_scr, halo_scr,
):
    yh = lax.axis_index("yh")
    core = lax.axis_index("core")
    frame = yh * 2 + core
    weights = [mix_ref[f, pl.ds(frame, 1), :] for f in range(4)]

    sums = tuple(jnp.zeros((8, C), F32) for _ in range(4))
    sources = [
        (ref, far, (yh if far == 0 else 1 - yh) * 320 + owner * 160)
        for ref, owner in ((own_ref, core), (other_ref, 1 - core))
        for far in range(2)
    ]

    def chunk(i, sums):
        start = pl.multiple_of(i * 32, 32)
        for ref, far, base in sources:
            at = pl.multiple_of(base + i * 32, 32)
            cots = [ref[pl.ds(far * 640 + f * 160 + start, 32), :].astype(F32) for f in range(4)]
            total = weights[0] * cots[0]
            for f in range(1, 4):
                total = total + weights[f] * cots[f]
            mg_scr[pl.ds(at, 32), :] = total.astype(LOW)
            mixed = mixed_ref[pl.ds(at, 32), :].astype(F32)
            sums = tuple(sums[f] + fold(mixed * cots[f]) for f in range(4))
        return sums

    sums = lax.fori_loop(0, 5, chunk, sums)

    halo_scr[...] = jnp.zeros_like(halo_scr)
    for index, ref in enumerate((own_ref, other_ref)):
        for far in range(2):
            for side in range(2):
                start = 1280 + far * 64 + side * 32
                group = ref[start : start + 32, :].astype(F32)
                total = weights[0] * group[0:5]
                for f in range(1, 4):
                    total = total + weights[f] * group[8 * f : 8 * f + 5]
                place = side * SIDE + far * 16 + index * 8
                halo_scr[place : place + 5, :] = total
    flipped = dot_plain(flip_matrix(maps_ref[0, 0, 0], maps_ref[0, 1, 0], yh, core), halo_scr[...].astype(LOW)).astype(LOW)
    edge_grad = dot_rows(flipped, point_ref[...]).astype(LOW).astype(F32)
    edge_scr[...] = jnp.zeros_like(edge_scr)
    valid = lax.broadcasted_iota(jnp.int32, (SIDE, C), 0) < TR
    for side in range(2):
        base = side * 48
        edge_scr[base + 8 : base + 8 + SIDE, :] = jnp.where(
            valid, edge_grad[side * SIDE : (side + 1) * SIDE, :], 0.0
        )
    for side in range(2):
        base = side * 48
        flip = maps_ref[0, side, 0] != 0
        total = jnp.zeros((24, C), F32)
        for row_off in range(3):
            plain = 3 * row_off + (2 if side == 0 else 0)
            turned = 3 * (2 - row_off) + (2 if side == 0 else 0)
            tap = jnp.where(flip, taps_ref[turned : turned + 1, :], taps_ref[plain : plain + 1, :])
            start = base + 9 - row_off
            total = total + tap * edge_scr[start : start + 24, :]
        halo_scr[side * SIDE : side * SIDE + 24, :] = total

    col = lax.broadcasted_iota(jnp.int32, (TC, C), 0)
    for part in range(4):
        grad = dot_rows(mg_scr[part * 160 : (part + 1) * 160, :], point_ref[...])
        sg_scr[1, 1 + 5 * part : 6 + 5 * part] = grad.astype(LOW).astype(F32).reshape(5, TC, C)
    for shift in range(3):
        for row in (0, TR + 1):
            sg_scr[shift, row] = jnp.zeros((TC, C), F32)

    def shift_and_taps(step, sums):
        for r in (2 * step, 2 * step + 1):
            sums = shift_row(r, sums)
        return sums

    def shift_row(r, sums):
        x = sg_scr[1, r + 1]
        sg_scr[0, r + 1] = jnp.where(col == TC - 1, 0.0, pltpu.roll(x, TC - 1, 0))
        sg_scr[2, r + 1] = jnp.where(col == 0, 0.0, pltpu.roll(x, 1, 0))
        return tuple(
            sums[k] + fold(x * wide_ref[k % 3, r + k // 3].astype(F32)) for k in range(9)
        )

    tap_sums = lax.fori_loop(
        0, TR // 2, shift_and_taps, tuple(jnp.zeros((8, C), F32) for _ in range(9))
    )

    def gradient(step, total):
        for r in (2 * step, 2 * step + 1):
            total = gradient_row(r, total)
        return total

    def gradient_row(r, total):
        acc = jnp.zeros((TC, C), F32)
        for row_off in range(3):
            for col_off in range(3):
                tap = taps_ref[row_off * 3 + col_off : row_off * 3 + col_off + 1, :]
                acc = acc + tap * sg_scr[col_off, r + 2 - row_off]
        acc = acc + jnp.where(col == 0, halo_scr[pl.ds(r, 1), :], 0.0)
        acc = acc + jnp.where(col == TC - 1, halo_scr[pl.ds(SIDE + r, 1), :], 0.0)
        rows = pl.ds(pl.multiple_of(r * TC, TC), TC)
        pre = ((mg_scr[rows, :].astype(F32) + acc) * slope_ref[rows, :]).astype(LOW)
        pre_ref[rows, :] = pre
        return total + fold(pre.astype(F32))

    bias_sum = lax.fori_loop(0, TR // 2, gradient, jnp.zeros((8, C), F32))

    tail = lax.broadcasted_iota(jnp.int32, (32, C), 0)
    total = jnp.zeros((32, C), F32)
    for f in range(4):
        total = jnp.where(tail == 4 * f + frame, jnp.sum(sums[f], axis=0, keepdims=True), total)
    for k in range(9):
        total = jnp.where(tail == 16 + k, jnp.sum(tap_sums[k], axis=0, keepdims=True), total)
    total = jnp.where(tail == 25, jnp.sum(bias_sum, axis=0, keepdims=True), total)

    def store(low_ref, high_ref):
        for part in range(3):
            rows = slice(part * C, (part + 1) * C)
            low_ref[rows, :] = dot_plain(rows_t_ref[rows, :], pre_ref[...]).astype(low_ref.dtype)
        kind = high_ref.dtype
        high_ref[0:C, :] = dot_plain(rows_t_ref[3 * C : 4 * C, :], pre_ref[...]).astype(kind)
        high_ref[C : 2 * C, :] = dot_plain(spread_t_ref[...], mg_scr[...]).astype(kind)
        high_ref[2 * C : 2 * C + 32, :] = total.astype(kind)
        high_ref[2 * C + 32 : 3 * C, :] = jnp.zeros((C - 32, C), kind)

    @pl.when(core == 0)
    def _():
        store(keep_ref, send_ref)

    @pl.when(core != 0)
    def _():
        store(send_ref, keep_ref)


def input_grad_kernel(pre_ref, w_ref, out_ref, wide_ref):
    step = PIXELS // 5
    for part in range(5):
        first = part * step
        for child in range(4):
            rows = dot_rows(pre_ref[first : first + step, :], w_ref[child * C : (child + 1) * C, :])
            for h in range(2):
                wide_ref[h, pl.ds(4 * first + child, step, stride=4), :] = rows[:, h * 128 : (h + 1) * 128]
    for h in range(2):
        out_ref[0, :, h * 128 : (h + 1) * 128] = wide_ref[h].astype(LOW)


def unpack_kernel(scale, low_ref, down_ref, bias_ref, taps_ref, point_ref, mix_ref):
    down_ref[...] = low_ref[0:1024, :].astype(F32) * scale
    point_ref[...] = low_ref[1024:1280, :].astype(F32) * scale
    tail = low_ref[1280:1312, :].astype(F32) * scale
    for f in range(4):
        mix_ref[f] = tail[4 * f : 4 * f + 4, :]
    taps_ref[...] = tail[16:25, :]
    bias_ref[...] = tail[25:26, :]


def shape(dims, dtype):
    return jax.ShapeDtypeStruct(dims, dtype)


SMEM_SPEC = pl.BlockSpec(memory_space=pltpu.SMEM)
VMEM_SPEC = pl.BlockSpec(memory_space=pltpu.VMEM)


def call(kernel, name, specs, outs, scratch=()):
    return pl.pallas_call(
        kernel,
        name=name,
        in_specs=specs,
        out_specs=jax.tree.map(lambda _: VMEM_SPEC, outs),
        out_shape=outs,
        scratch_shapes=list(scratch),
        compiler_params=pltpu.CompilerParams(vmem_limit_bytes=VMEM_BYTES),
    )


def scatter_sum(rows, axis):
    count = lax.axis_size(axis)
    low = rows.astype(LOW).reshape(count, rows.shape[0] // count, C)
    got = lax.all_to_all(low, axis, split_axis=0, concat_axis=0, tiled=True)
    return jnp.sum(got.astype(F32), axis=0)


def copies(rows, axis):
    count = lax.axis_size(axis)
    wide = jnp.broadcast_to(rows[None], (count,) + rows.shape)
    return lax.all_to_all(wide, axis, split_axis=0, concat_axis=0, tiled=True)


def sum_over_devices(keep, send):
    got = lax.ppermute(send, "core", [(0, 1), (1, 0)])
    rows = keep + got.astype(F32)
    rows = scatter_sum(rows, ("x", "z"))
    rows = jnp.sum(copies(rows.astype(LOW), ("yh", "yl")).astype(F32), axis=0)
    rows = copies(rows.astype(LOW), ("x", "z")).reshape(-1, C)
    return lax.all_gather(rows, "core", axis=0, tiled=True)


def on_device(
    activations, down_weight, down_bias, taps, point_weight, time_mix, edge_rows, cotangent
):
    frames = cotangent.shape[0]
    tiles = lax.axis_size(PIX)
    scale = 1.0 / math.sqrt(frames * tiles * PIXELS)
    swap = [(0, 1), (1, 0)]
    far_half = lax.ppermute(cotangent, "yh", swap)

    act_cols = activations.reshape(TR, 4 * TC, C)
    cot_cols = cotangent.reshape(frames, TR // frames, TC, C)
    even = lax.axis_index("yl") % 2 == 0
    west_act = act_cols[:, :4, :].reshape(4 * TR, C)
    east_act = act_cols[:, 4 * TC - 4 :, :].reshape(4 * TR, C)
    west_cot = cot_cols[:, :, 0, :].reshape(TR, C)
    east_cot = cot_cols[:, :, TC - 1, :].reshape(TR, C)

    def exchange(west, east, axes, hops):
        first = lax.ppermute(jnp.where(even, east, west), axes, hops(lambda i: i ^ 1))
        second = lax.ppermute(
            jnp.where(even, west, east), axes, hops(lambda i: (i + 2 * (i % 2) - 1) % tiles)
        )
        return jnp.where(even, second, first), jnp.where(even, first, second)

    from_west, from_east = exchange(
        jnp.concatenate([west_act, west_cot], axis=0),
        jnp.concatenate([east_act, east_cot], axis=0),
        PIX,
        lambda partner: [(i, partner(i)) for i in range(tiles)],
    )
    cross = exchange(
        west_cot,
        east_cot,
        ("yh",) + PIX,
        lambda partner: [
            (y * tiles + i, (1 - y) * tiles + partner(i)) for y in range(2) for i in range(tiles)
        ],
    )
    bias = down_bias.reshape(1, C)
    rows_t, pooled, slope = call(
        forward_kernel,
        "forward",
        [VMEM_SPEC] * 3,
        (shape((4 * C, PIXELS), LOW), shape((PIXELS, C), LOW), shape((PIXELS, C), F32)),
        [
            pltpu.VMEM((2, 4 * PIXELS, 128), F32),
        ],
    )(activations.reshape(4 * PIXELS, C), down_weight, bias)
    from_west, from_east, cross, pooled = lax.optimization_barrier(
        (from_west, from_east, cross, pooled)
    )
    edge_act = jnp.stack([from_west[: 4 * TR], from_east[: 4 * TR]])
    edge_pair = jnp.pad(
        jnp.stack([from_west[4 * TR :], from_east[4 * TR :], *cross]).reshape(
            4 * frames, TR // frames, C
        ),
        ((0, 0), (0, 3), (0, 0)),
    ).reshape(16 * 8, C)
    own = jnp.concatenate(
        [cotangent.reshape(PIXELS, C), far_half.reshape(PIXELS, C), edge_pair], axis=0
    )
    other = lax.ppermute(own, "core", swap)
    wide, spread_t, mixed = call(
        spread_kernel,
        "spread",
        [SMEM_SPEC] + [VMEM_SPEC] * 6,
        (shape((3, TR + 2, TC, C), LOW), shape((C, PIXELS), LOW), shape((PIXELS, C), LOW)),
        [
            pltpu.VMEM((2, 8 * SIDE, 128), F32),
            pltpu.VMEM((2 * SIDE, C), F32),
            pltpu.VMEM((3, TR + 2, TC, C), F32),
            pltpu.VMEM((PIXELS, C), LOW),
        ],
    )(edge_rows, edge_act, down_weight, bias, taps, point_weight, pooled)
    keep, send, pre = call(
        backward_kernel,
        "backward",
        [SMEM_SPEC] + [VMEM_SPEC] * 10,
        (shape((PAD_ROWS // 2, C), F32), shape((PAD_ROWS // 2, C), LOW), shape((PIXELS, C), LOW)),
        [
            pltpu.VMEM((PIXELS, C), LOW),
            pltpu.VMEM((3, TR + 2, TC, C), F32),
            pltpu.VMEM((96, C), F32),
            pltpu.VMEM((2 * SIDE, C), F32),
        ],
    )(edge_rows, own, other, time_mix, point_weight, taps, wide, spread_t, mixed, slope, rows_t)
    grad_input = call(
        input_grad_kernel,
        "input_grad",
        [VMEM_SPEC] * 2,
        shape((1, 4 * PIXELS, C), LOW),
        [pltpu.VMEM((2, 4 * PIXELS, 128), F32)],
    )(pre, down_weight)
    total = sum_over_devices(keep, send)
    grad_down, grad_bias, grad_taps, grad_point, grad_mix = call(
        functools.partial(unpack_kernel, scale),
        "unpack",
        [VMEM_SPEC],
        (
            shape((4 * C, C), F32),
            shape((1, C), F32),
            shape((9, C), F32),
            shape((C, C), F32),
            shape((frames, frames, C), F32),
        ),
    )(total)
    return grad_input, grad_down, grad_bias.reshape(C), grad_taps, grad_point, grad_mix


def solution(mesh):
    yl = mesh.shape["pix"] // 32 if mesh.shape["pix"] >= 128 else 2
    x, z = (4, 8) if mesh.shape["pix"] >= 128 else (2, 2)
    chips = Mesh(mesh.devices.reshape(2, 2, x, z, yl), ("yh", "core", "x", "z", "yl"))
    in_specs = (
        P(TM, PIX, None),
        P(),
        P(),
        P(),
        P(),
        P(),
        P(PIX, None, None),
        P(None, PIX + TM, None),
    )
    out_specs = (P(TM, PIX, None), P(), P(), P(), P(), P())
    return jax.shard_map(
        on_device, mesh=chips, in_specs=in_specs, out_specs=out_specs, check_vma=False
    )
```

```python
import functools
import math

import jax
import jax.numpy as jnp
from jax import lax
from jax.experimental import pallas as pl
from jax.experimental.pallas import tpu as pltpu
from jax.sharding import Mesh, PartitionSpec as P

C = 256
TR = 20
TC = 32
PIXELS = TR * TC
SIDE = 32
TM = ("yh", "core")
PIX = ("x", "z", "yl")
HALF = 672
LOW = jnp.bfloat16
F32 = jnp.float32
VMEM_BYTES = 24 << 20


def dot_plain(a, b):
    return jnp.dot(a, b, preferred_element_type=F32)


def dot_rows(a, b):
    return lax.dot_general(a, b, (((1,), (1,)), ((), ())), preferred_element_type=F32)


def every_fourth(ref, first, count):
    return jnp.concatenate([ref[h, pl.ds(first, count, stride=4), :] for h in range(2)], axis=1)


def forward_kernel(act_ref, w_ref, bias_ref, rows_t_ref, pooled_ref, slope_ref, wide_ref):
    step = PIXELS // 5
    for part in range(5):
        first = part * step
        span = slice(4 * first, 4 * first + 4 * step)
        for h in range(2):
            wide_ref[h, span, :] = act_ref[span, h * 128 : (h + 1) * 128].astype(F32)
        total = bias_ref[...]
        for child in range(4):
            rows = every_fourth(wide_ref, 4 * first + child, step).astype(LOW)
            total = total + dot_plain(rows, w_ref[child * C : (child + 1) * C, :])
            rows_t_ref[child * C : (child + 1) * C, first : first + step] = rows.T
        sigma = jax.nn.sigmoid(total)
        pooled_ref[first : first + step, :] = (total * sigma).astype(LOW)
        slope_ref[first : first + step, :] = sigma * (1.0 + total * (1.0 - sigma))


def flip_matrix(west_flip, east_flip, yh=None, core=None):
    row = lax.broadcasted_iota(jnp.int32, (2 * SIDE, 2 * SIDE), 0)
    col = lax.broadcasted_iota(jnp.int32, (2 * SIDE, 2 * SIDE), 1)
    east = row >= SIDE
    base = jnp.where(east, SIDE, 0)
    local = row - base
    flip = jnp.where(east, east_flip, west_flip)
    local = jnp.where(flip != 0, TR - 1 - local, local)
    if yh is not None:
        place = (local >= 10).astype(jnp.int32)
        rest = local - 10 * place
        other = (rest >= 5).astype(jnp.int32)
        local = jnp.where(place == yh, 0, 16) + jnp.where(other == core, 0, 8) + rest - 5 * other
    source = base + local
    return (col == source).astype(F32).astype(LOW)


def spread_kernel(
    maps_ref, edge_ref, w_ref, bias_ref, taps_ref, point_ref, pooled_ref,
    wide_low_ref, spread_t_ref, mixed_ref, edge_scr, halo_scr, wide_scr, spread_scr,
):
    edge_scr[...] = jnp.zeros_like(edge_scr)
    for side in range(2):
        for h in range(2):
            edge_scr[h, 4 * SIDE * side : 4 * SIDE * side + 4 * TR, :] = edge_ref[
                side, :, h * 128 : (h + 1) * 128
            ].astype(F32)
    total = bias_ref[...]
    for child in range(4):
        rows = every_fourth(edge_scr, child, 2 * SIDE).astype(LOW)
        total = total + dot_plain(rows, w_ref[child * C : (child + 1) * C, :])
    halo = (total * jax.nn.sigmoid(total)).astype(LOW)
    halo_scr[...] = dot_plain(flip_matrix(maps_ref[0, 0, 0], maps_ref[0, 1, 0]), halo)
    col = lax.broadcasted_iota(jnp.int32, (TC, C), 0)
    for shift in range(3):
        for row in (0, TR + 1):
            wide_scr[shift, row] = jnp.zeros((TC, C), F32)
            wide_low_ref[shift, row] = jnp.zeros((TC, C), LOW)

    def widen(step, carry):
        for r in (2 * step, 2 * step + 1):
            widen_row(r)
        return carry

    def widen_row(r):
        x = pooled_ref[pl.ds(pl.multiple_of(r * TC, TC), TC), :].astype(F32)
        left = jnp.where(col == 0, halo_scr[pl.ds(r, 1), :], pltpu.roll(x, 1, 0))
        right = jnp.where(col == TC - 1, halo_scr[pl.ds(SIDE + r, 1), :], pltpu.roll(x, TC - 1, 0))
        for shift, value in enumerate((left, x, right)):
            wide_scr[shift, r + 1] = value
            wide_low_ref[shift, r + 1] = value.astype(LOW)

    lax.fori_loop(0, TR // 2, widen, 0)

    def convolve(step, carry):
        for r in (2 * step, 2 * step + 1):
            convolve_row(r)
        return carry

    def convolve_row(r):
        acc = jnp.zeros((TC, C), F32)
        for row_off in range(3):
            for col_off in range(3):
                tap = taps_ref[row_off * 3 + col_off : row_off * 3 + col_off + 1, :]
                acc = acc + tap * wide_scr[col_off, r + row_off]
        spread_scr[pl.ds(pl.multiple_of(r * TC, TC), TC), :] = acc.astype(LOW)

    lax.fori_loop(0, TR // 2, convolve, 0)
    step = PIXELS // 5
    for part in range(5):
        span = slice(part * step, (part + 1) * step)
        rows = spread_scr[span, :]
        mixed_ref[span, :] = (pooled_ref[span, :].astype(F32) + dot_plain(rows, point_ref[...])).astype(LOW)
        spread_t_ref[:, span] = rows.T


def fold(x):
    return jnp.sum(x.reshape(x.shape[0] // 8, 8, C), axis=0)


def backward_kernel(
    maps_ref, own_ref, other_ref, mix_ref, point_ref, taps_ref, wide_ref, spread_t_ref,
    mixed_ref, slope_ref, rows_t_ref,
    send_ref, pre_ref, mg_ref, small_ref, sg_scr, edge_scr, halo_scr,
):
    yh = lax.axis_index("yh")
    core = lax.axis_index("core")
    frame = yh * 2 + core
    weights = [mix_ref[f, pl.ds(frame, 1), :] for f in range(4)]

    sums = tuple(jnp.zeros((8, C), F32) for _ in range(4))
    sources = [
        (ref, far, (yh if far == 0 else 1 - yh) * 320 + owner * 160)
        for ref, owner in ((own_ref, core), (other_ref, 1 - core))
        for far in range(2)
    ]

    def chunk(i, sums):
        start = pl.multiple_of(i * 32, 32)
        for ref, far, base in sources:
            at = pl.multiple_of(base + i * 32, 32)
            cots = [ref[pl.ds(far * 640 + f * 160 + start, 32), :].astype(F32) for f in range(4)]
            total = weights[0] * cots[0]
            for f in range(1, 4):
                total = total + weights[f] * cots[f]
            mg_ref[pl.ds(at, 32), :] = total.astype(LOW)
            mixed = mixed_ref[pl.ds(at, 32), :].astype(F32)
            sums = tuple(sums[f] + fold(mixed * cots[f]) for f in range(4))
        return sums

    sums = lax.fori_loop(0, 5, chunk, sums)

    halo_scr[...] = jnp.zeros_like(halo_scr)
    for index, ref in enumerate((own_ref, other_ref)):
        for far in range(2):
            for side in range(2):
                start = 1280 + far * 64 + side * 32
                group = ref[start : start + 32, :].astype(F32)
                total = weights[0] * group[0:5]
                for f in range(1, 4):
                    total = total + weights[f] * group[8 * f : 8 * f + 5]
                place = side * SIDE + far * 16 + index * 8
                halo_scr[place : place + 5, :] = total
    flipped = dot_plain(flip_matrix(maps_ref[0, 0, 0], maps_ref[0, 1, 0], yh, core), halo_scr[...].astype(LOW)).astype(LOW)
    edge_grad = dot_rows(flipped, point_ref[...]).astype(LOW).astype(F32)
    edge_scr[...] = jnp.zeros_like(edge_scr)
    valid = lax.broadcasted_iota(jnp.int32, (SIDE, C), 0) < TR
    for side in range(2):
        base = side * 48
        edge_scr[base + 8 : base + 8 + SIDE, :] = jnp.where(
            valid, edge_grad[side * SIDE : (side + 1) * SIDE, :], 0.0
        )
    for side in range(2):
        base = side * 48
        flip = maps_ref[0, side, 0] != 0
        total = jnp.zeros((24, C), F32)
        for row_off in range(3):
            plain = 3 * row_off + (2 if side == 0 else 0)
            turned = 3 * (2 - row_off) + (2 if side == 0 else 0)
            tap = jnp.where(flip, taps_ref[turned : turned + 1, :], taps_ref[plain : plain + 1, :])
            start = base + 9 - row_off
            total = total + tap * edge_scr[start : start + 24, :]
        halo_scr[side * SIDE : side * SIDE + 24, :] = total

    col = lax.broadcasted_iota(jnp.int32, (TC, C), 0)
    for part in range(4):
        grad = dot_rows(mg_ref[part * 160 : (part + 1) * 160, :], point_ref[...])
        sg_scr[1, 1 + 5 * part : 6 + 5 * part] = grad.astype(LOW).astype(F32).reshape(5, TC, C)
    for shift in range(3):
        for row in (0, TR + 1):
            sg_scr[shift, row] = jnp.zeros((TC, C), F32)

    def shift_and_taps(step, sums):
        for r in (2 * step, 2 * step + 1):
            sums = shift_row(r, sums)
        return sums

    def shift_row(r, sums):
        x = sg_scr[1, r + 1]
        sg_scr[0, r + 1] = jnp.where(col == TC - 1, 0.0, pltpu.roll(x, TC - 1, 0))
        sg_scr[2, r + 1] = jnp.where(col == 0, 0.0, pltpu.roll(x, 1, 0))
        return tuple(
            sums[k] + fold(x * wide_ref[k % 3, r + k // 3].astype(F32)) for k in range(9)
        )

    tap_sums = lax.fori_loop(
        0, TR // 2, shift_and_taps, tuple(jnp.zeros((8, C), F32) for _ in range(9))
    )

    def gradient(step, total):
        for r in (2 * step, 2 * step + 1):
            total = gradient_row(r, total)
        return total

    def gradient_row(r, total):
        acc = jnp.zeros((TC, C), F32)
        for row_off in range(3):
            for col_off in range(3):
                tap = taps_ref[row_off * 3 + col_off : row_off * 3 + col_off + 1, :]
                acc = acc + tap * sg_scr[col_off, r + 2 - row_off]
        acc = acc + jnp.where(col == 0, halo_scr[pl.ds(r, 1), :], 0.0)
        acc = acc + jnp.where(col == TC - 1, halo_scr[pl.ds(SIDE + r, 1), :], 0.0)
        rows = pl.ds(pl.multiple_of(r * TC, TC), TC)
        pre = ((mg_ref[rows, :].astype(F32) + acc) * slope_ref[rows, :]).astype(LOW)
        pre_ref[rows, :] = pre
        return total + fold(pre.astype(F32))

    bias_sum = lax.fori_loop(0, TR // 2, gradient, jnp.zeros((8, C), F32))

    tail = lax.broadcasted_iota(jnp.int32, (32, C), 0)
    total = jnp.zeros((32, C), F32)
    for f in range(4):
        total = jnp.where(tail == 4 * f + frame, jnp.sum(sums[f], axis=0, keepdims=True), total)
    for k in range(9):
        total = jnp.where(tail == 16 + k, jnp.sum(tap_sums[k], axis=0, keepdims=True), total)
    total = jnp.where(tail == 25, jnp.sum(bias_sum, axis=0, keepdims=True), total)

    small_ref[...] = total

    @pl.when(core == 0)
    def _():
        store_high(send_ref, rows_t_ref, spread_t_ref, pre_ref, mg_ref, small_ref)

    @pl.when(core != 0)
    def _():
        store_low(send_ref, rows_t_ref, pre_ref)


def put(ref, first, value):
    value = value.astype(ref.dtype)
    ref[first : first + value.shape[0], :] = value[:, :128]
    ref[HALF + first : HALF + first + value.shape[0], :] = value[:, 128:]


def store_low(ref, rows_t_ref, pre_ref):
    for first, count in ((0, 256), (256, 256), (512, 160)):
        put(ref, first, dot_plain(rows_t_ref[first : first + count, :], pre_ref[...]))


def store_high(ref, rows_t_ref, spread_t_ref, pre_ref, mg_ref, small_ref):
    for first, count in ((672, 160), (832, 192)):
        put(ref, first - HALF, dot_plain(rows_t_ref[first : first + count, :], pre_ref[...]))
    put(ref, 352, dot_plain(spread_t_ref[...], mg_ref[...]))
    put(ref, 608, small_ref[...])
    put(ref, 640, jnp.zeros((32, C), F32))


def keep_kernel(rows_t_ref, spread_t_ref, pre_ref, mg_ref, small_ref, keep_ref):
    core = lax.axis_index("core")

    @pl.when(core == 0)
    def _():
        store_low(keep_ref, rows_t_ref, pre_ref)

    @pl.when(core != 0)
    def _():
        store_high(keep_ref, rows_t_ref, spread_t_ref, pre_ref, mg_ref, small_ref)


def input_grad_kernel(pre_ref, w_ref, out_ref, wide_ref):
    step = PIXELS // 5
    for part in range(5):
        first = part * step
        for child in range(4):
            rows = dot_rows(pre_ref[first : first + step, :], w_ref[child * C : (child + 1) * C, :])
            for h in range(2):
                wide_ref[h, pl.ds(4 * first + child, step, stride=4), :] = rows[:, h * 128 : (h + 1) * 128]
    for h in range(2):
        out_ref[0, :, h * 128 : (h + 1) * 128] = wide_ref[h].astype(LOW)


def unpack_kernel(scale, low_ref, down_ref, bias_ref, taps_ref, point_ref, mix_ref):
    def take(first, count, side):
        start = first + side * HALF
        return low_ref[start : start + count, :].astype(F32) * scale

    for side in range(2):
        cols = slice(side * 128, side * 128 + 128)
        down_ref[0:HALF, cols] = take(0, HALF, side)
        down_ref[HALF:1024, cols] = take(2 * HALF, 352, side)
        point_ref[:, cols] = take(2 * HALF + 352, C, side)
        tail = take(2 * HALF + 608, 32, side)
        for f in range(4):
            mix_ref[f, :, cols] = tail[4 * f : 4 * f + 4, :]
        taps_ref[:, cols] = tail[16:25, :]
        bias_ref[:, cols] = tail[25:26, :]


def shape(dims, dtype):
    return jax.ShapeDtypeStruct(dims, dtype)


SMEM_SPEC = pl.BlockSpec(memory_space=pltpu.SMEM)
VMEM_SPEC = pl.BlockSpec(memory_space=pltpu.VMEM)


def call(kernel, name, specs, outs, scratch=()):
    return pl.pallas_call(
        kernel,
        name=name,
        in_specs=specs,
        out_specs=jax.tree.map(lambda _: VMEM_SPEC, outs),
        out_shape=outs,
        scratch_shapes=list(scratch),
        compiler_params=pltpu.CompilerParams(vmem_limit_bytes=VMEM_BYTES),
    )


def exchange_copies(chunk, axis):
    count = lax.axis_size(axis)
    wide = jnp.broadcast_to(chunk.astype(LOW)[None], (count,) + chunk.shape)
    return lax.all_to_all(wide, axis, split_axis=0, concat_axis=0, tiled=True)


def sum_over_devices(keep, send):
    got = lax.ppermute(send, "core", [(0, 1), (1, 0)])
    rows = (keep + got.astype(F32)).astype(LOW).reshape(lax.axis_size(("x", "z")), -1, 2, 128)
    got = lax.all_to_all(rows, ("x", "z"), split_axis=0, concat_axis=0, tiled=True)
    chunk = jnp.sum(got.astype(F32), axis=0)
    chunk = jnp.sum(exchange_copies(chunk, ("yh", "yl")).astype(F32), axis=0)
    rows = exchange_copies(chunk, ("x", "z")).reshape(2 * HALF, 128)
    return lax.all_gather(rows, "core", axis=0, tiled=True)


def on_device(
    activations, down_weight, down_bias, taps, point_weight, time_mix, edge_rows, cotangent
):
    frames = cotangent.shape[0]
    tiles = lax.axis_size(PIX)
    scale = 1.0 / math.sqrt(frames * tiles * PIXELS)
    swap = [(0, 1), (1, 0)]
    far_half = lax.ppermute(cotangent, "yh", swap)

    act_cols = activations.reshape(TR, 4 * TC, C)
    cot_cols = cotangent.reshape(frames, TR // frames, TC, C)
    even = lax.axis_index("yl") % 2 == 0
    west_act = act_cols[:, :4, :].reshape(4 * TR, C)
    east_act = act_cols[:, 4 * TC - 4 :, :].reshape(4 * TR, C)
    west_cot = cot_cols[:, :, 0, :].reshape(TR, C)
    east_cot = cot_cols[:, :, TC - 1, :].reshape(TR, C)

    def exchange(west, east, axes, hops):
        first = lax.ppermute(jnp.where(even, east, west), axes, hops(lambda i: i ^ 1))
        second = lax.ppermute(
            jnp.where(even, west, east), axes, hops(lambda i: (i + 2 * (i % 2) - 1) % tiles)
        )
        return jnp.where(even, second, first), jnp.where(even, first, second)

    from_west, from_east = exchange(
        jnp.concatenate([west_act, west_cot], axis=0),
        jnp.concatenate([east_act, east_cot], axis=0),
        PIX,
        lambda partner: [(i, partner(i)) for i in range(tiles)],
    )
    cross = exchange(
        west_cot,
        east_cot,
        ("yh",) + PIX,
        lambda partner: [
            (y * tiles + i, (1 - y) * tiles + partner(i)) for y in range(2) for i in range(tiles)
        ],
    )
    bias = down_bias.reshape(1, C)
    rows_t, pooled, slope = call(
        forward_kernel,
        "forward",
        [VMEM_SPEC] * 3,
        (shape((4 * C, PIXELS), LOW), shape((PIXELS, C), LOW), shape((PIXELS, C), F32)),
        [
            pltpu.VMEM((2, 4 * PIXELS, 128), F32),
        ],
    )(activations.reshape(4 * PIXELS, C), down_weight, bias)
    from_west, from_east, cross, pooled = lax.optimization_barrier(
        (from_west, from_east, cross, pooled)
    )
    edge_act = jnp.stack([from_west[: 4 * TR], from_east[: 4 * TR]])
    edge_pair = jnp.pad(
        jnp.stack([from_west[4 * TR :], from_east[4 * TR :], *cross]).reshape(
            4 * frames, TR // frames, C
        ),
        ((0, 0), (0, 3), (0, 0)),
    ).reshape(16 * 8, C)
    own = jnp.concatenate(
        [cotangent.reshape(PIXELS, C), far_half.reshape(PIXELS, C), edge_pair], axis=0
    )
    other = lax.ppermute(own, "core", swap)
    wide, spread_t, mixed = call(
        spread_kernel,
        "spread",
        [SMEM_SPEC] + [VMEM_SPEC] * 6,
        (shape((3, TR + 2, TC, C), LOW), shape((C, PIXELS), LOW), shape((PIXELS, C), LOW)),
        [
            pltpu.VMEM((2, 8 * SIDE, 128), F32),
            pltpu.VMEM((2 * SIDE, C), F32),
            pltpu.VMEM((3, TR + 2, TC, C), F32),
            pltpu.VMEM((PIXELS, C), LOW),
        ],
    )(edge_rows, edge_act, down_weight, bias, taps, point_weight, pooled)
    send, pre, mixed_grad, small = call(
        backward_kernel,
        "backward",
        [SMEM_SPEC] + [VMEM_SPEC] * 10,
        (
            shape((2 * HALF, 128), LOW),
            shape((PIXELS, C), LOW),
            shape((PIXELS, C), LOW),
            shape((32, C), F32),
        ),
        [
            pltpu.VMEM((3, TR + 2, TC, C), F32),
            pltpu.VMEM((96, C), F32),
            pltpu.VMEM((2 * SIDE, C), F32),
        ],
    )(edge_rows, own, other, time_mix, point_weight, taps, wide, spread_t, mixed, slope, rows_t)
    keep = call(keep_kernel, "keep", [VMEM_SPEC] * 5, shape((2 * HALF, 128), F32))(
        rows_t, spread_t, pre, mixed_grad, small
    )
    grad_input = call(
        input_grad_kernel,
        "input_grad",
        [VMEM_SPEC] * 2,
        shape((1, 4 * PIXELS, C), LOW),
        [pltpu.VMEM((2, 4 * PIXELS, 128), F32)],
    )(pre, down_weight)
    total = sum_over_devices(keep, send)
    grad_down, grad_bias, grad_taps, grad_point, grad_mix = call(
        functools.partial(unpack_kernel, scale),
        "unpack",
        [VMEM_SPEC],
        (
            shape((4 * C, C), F32),
            shape((1, C), F32),
            shape((9, C), F32),
            shape((C, C), F32),
            shape((frames, frames, C), F32),
        ),
    )(total)
    return grad_input, grad_down, grad_bias.reshape(C), grad_taps, grad_point, grad_mix


def solution(mesh):
    yl = mesh.shape["pix"] // 32 if mesh.shape["pix"] >= 128 else 2
    x, z = (4, 8) if mesh.shape["pix"] >= 128 else (2, 2)
    chips = Mesh(mesh.devices.reshape(2, 2, x, z, yl), ("yh", "core", "x", "z", "yl"))
    in_specs = (
        P(TM, PIX, None),
        P(),
        P(),
        P(),
        P(),
        P(),
        P(PIX, None, None),
        P(None, PIX + TM, None),
    )
    out_specs = (P(TM, PIX, None), P(), P(), P(), P(), P())
    return jax.shard_map(
        on_device, mesh=chips, in_specs=in_specs, out_specs=out_specs, check_vma=False
    )
```

```python
import functools
import math

import jax
import jax.numpy as jnp
from jax import lax
from jax.experimental import pallas as pl
from jax.experimental.pallas import tpu as pltpu
from jax.sharding import Mesh, PartitionSpec as P

C = 256
TR = 20
TC = 32
PIXELS = TR * TC
SIDE = 32
TM = ("yh", "core")
PIX = ("x", "z", "yl")
HALF = 672
STEP_ROWS = 4
LOW = jnp.bfloat16
F32 = jnp.float32
VMEM_BYTES = 24 << 20


def dot_plain(a, b):
    return jnp.dot(a, b, preferred_element_type=F32)


def dot_rows(a, b):
    return lax.dot_general(a, b, (((1,), (1,)), ((), ())), preferred_element_type=F32)


def every_fourth(ref, first, count):
    return jnp.concatenate([ref[h, pl.ds(first, count, stride=4), :] for h in range(2)], axis=1)


def forward_kernel(act_ref, w_ref, bias_ref, rows_t_ref, pooled_ref, slope_ref, wide_ref):
    step = PIXELS // 5
    for part in range(5):
        first = part * step
        span = slice(4 * first, 4 * first + 4 * step)
        for h in range(2):
            wide_ref[h, span, :] = act_ref[span, h * 128 : (h + 1) * 128].astype(F32)
        total = bias_ref[...]
        for child in range(4):
            rows = every_fourth(wide_ref, 4 * first + child, step).astype(LOW)
            total = total + dot_plain(rows, w_ref[child * C : (child + 1) * C, :])
            rows_t_ref[child * C : (child + 1) * C, first : first + step] = rows.T
        sigma = jax.nn.sigmoid(total)
        pooled_ref[first : first + step, :] = (total * sigma).astype(LOW)
        slope_ref[first : first + step, :] = sigma * (1.0 + total * (1.0 - sigma))


def flip_matrix(west_flip, east_flip, yh=None, core=None):
    row = lax.broadcasted_iota(jnp.int32, (2 * SIDE, 2 * SIDE), 0)
    col = lax.broadcasted_iota(jnp.int32, (2 * SIDE, 2 * SIDE), 1)
    east = row >= SIDE
    base = jnp.where(east, SIDE, 0)
    local = row - base
    flip = jnp.where(east, east_flip, west_flip)
    local = jnp.where(flip != 0, TR - 1 - local, local)
    if yh is not None:
        place = (local >= 10).astype(jnp.int32)
        rest = local - 10 * place
        other = (rest >= 5).astype(jnp.int32)
        local = jnp.where(place == yh, 0, 16) + jnp.where(other == core, 0, 8) + rest - 5 * other
    source = base + local
    return (col == source).astype(F32).astype(LOW)


def spread_kernel(
    maps_ref, edge_ref, w_ref, bias_ref, taps_ref, point_ref, pooled_ref,
    wide_low_ref, spread_t_ref, mixed_ref, edge_scr, halo_scr, wide_scr, spread_scr,
):
    edge_scr[...] = jnp.zeros_like(edge_scr)
    for side in range(2):
        for h in range(2):
            edge_scr[h, 4 * SIDE * side : 4 * SIDE * side + 4 * TR, :] = edge_ref[
                side, :, h * 128 : (h + 1) * 128
            ].astype(F32)
    total = bias_ref[...]
    for child in range(4):
        rows = every_fourth(edge_scr, child, 2 * SIDE).astype(LOW)
        total = total + dot_plain(rows, w_ref[child * C : (child + 1) * C, :])
    halo = (total * jax.nn.sigmoid(total)).astype(LOW)
    halo_scr[...] = dot_plain(flip_matrix(maps_ref[0, 0, 0], maps_ref[0, 1, 0]), halo)
    col = lax.broadcasted_iota(jnp.int32, (TC, C), 0)
    for shift in range(3):
        for row in (0, TR + 1):
            wide_scr[shift, row] = jnp.zeros((TC, C), F32)
            wide_low_ref[shift, row] = jnp.zeros((TC, C), LOW)

    def widen(step, carry):
        for r in [STEP_ROWS * step + k for k in range(STEP_ROWS)]:
            widen_row(r)
        return carry

    def widen_row(r):
        x = pooled_ref[pl.ds(pl.multiple_of(r * TC, TC), TC), :].astype(F32)
        left = jnp.where(col == 0, halo_scr[pl.ds(r, 1), :], pltpu.roll(x, 1, 0))
        right = jnp.where(col == TC - 1, halo_scr[pl.ds(SIDE + r, 1), :], pltpu.roll(x, TC - 1, 0))
        for shift, value in enumerate((left, x, right)):
            wide_scr[shift, r + 1] = value
            wide_low_ref[shift, r + 1] = value.astype(LOW)

    lax.fori_loop(0, TR // STEP_ROWS, widen, 0)

    def convolve(step, carry):
        for r in [STEP_ROWS * step + k for k in range(STEP_ROWS)]:
            convolve_row(r)
        return carry

    def convolve_row(r):
        acc = jnp.zeros((TC, C), F32)
        for row_off in range(3):
            for col_off in range(3):
                tap = taps_ref[row_off * 3 + col_off : row_off * 3 + col_off + 1, :]
                acc = acc + tap * wide_scr[col_off, r + row_off]
        spread_scr[pl.ds(pl.multiple_of(r * TC, TC), TC), :] = acc.astype(LOW)

    lax.fori_loop(0, TR // STEP_ROWS, convolve, 0)
    step = PIXELS // 5
    for part in range(5):
        span = slice(part * step, (part + 1) * step)
        rows = spread_scr[span, :]
        mixed_ref[span, :] = (pooled_ref[span, :].astype(F32) + dot_plain(rows, point_ref[...])).astype(LOW)
        spread_t_ref[:, span] = rows.T


def fold(x):
    return jnp.sum(x.reshape(x.shape[0] // 8, 8, C), axis=0)


def backward_kernel(
    maps_ref, own_ref, other_ref, mix_ref, point_ref, taps_ref, wide_ref, spread_t_ref,
    mixed_ref, slope_ref, rows_t_ref,
    send_ref, pre_ref, mg_ref, small_ref, sg_scr, edge_scr, halo_scr,
):
    yh = lax.axis_index("yh")
    core = lax.axis_index("core")
    frame = yh * 2 + core
    weights = [mix_ref[f, pl.ds(frame, 1), :] for f in range(4)]

    sums = tuple(jnp.zeros((8, C), F32) for _ in range(4))
    sources = [
        (ref, far, (yh if far == 0 else 1 - yh) * 320 + owner * 160)
        for ref, owner in ((own_ref, core), (other_ref, 1 - core))
        for far in range(2)
    ]

    def chunk(i, sums):
        start = pl.multiple_of(i * 32, 32)
        for ref, far, base in sources:
            at = pl.multiple_of(base + i * 32, 32)
            cots = [ref[pl.ds(far * 640 + f * 160 + start, 32), :].astype(F32) for f in range(4)]
            total = weights[0] * cots[0]
            for f in range(1, 4):
                total = total + weights[f] * cots[f]
            mg_ref[pl.ds(at, 32), :] = total.astype(LOW)
            mixed = mixed_ref[pl.ds(at, 32), :].astype(F32)
            sums = tuple(sums[f] + fold(mixed * cots[f]) for f in range(4))
        return sums

    sums = lax.fori_loop(0, 5, chunk, sums)

    halo_scr[...] = jnp.zeros_like(halo_scr)
    for index, ref in enumerate((own_ref, other_ref)):
        for far in range(2):
            for side in range(2):
                start = 1280 + far * 64 + side * 32
                group = ref[start : start + 32, :].astype(F32)
                total = weights[0] * group[0:5]
                for f in range(1, 4):
                    total = total + weights[f] * group[8 * f : 8 * f + 5]
                place = side * SIDE + far * 16 + index * 8
                halo_scr[place : place + 5, :] = total
    flipped = dot_plain(flip_matrix(maps_ref[0, 0, 0], maps_ref[0, 1, 0], yh, core), halo_scr[...].astype(LOW)).astype(LOW)
    edge_grad = dot_rows(flipped, point_ref[...]).astype(LOW).astype(F32)
    edge_scr[...] = jnp.zeros_like(edge_scr)
    valid = lax.broadcasted_iota(jnp.int32, (SIDE, C), 0) < TR
    for side in range(2):
        base = side * 48
        edge_scr[base + 8 : base + 8 + SIDE, :] = jnp.where(
            valid, edge_grad[side * SIDE : (side + 1) * SIDE, :], 0.0
        )
    for side in range(2):
        base = side * 48
        flip = maps_ref[0, side, 0] != 0
        total = jnp.zeros((24, C), F32)
        for row_off in range(3):
            plain = 3 * row_off + (2 if side == 0 else 0)
            turned = 3 * (2 - row_off) + (2 if side == 0 else 0)
            tap = jnp.where(flip, taps_ref[turned : turned + 1, :], taps_ref[plain : plain + 1, :])
            start = base + 9 - row_off
            total = total + tap * edge_scr[start : start + 24, :]
        halo_scr[side * SIDE : side * SIDE + 24, :] = total

    col = lax.broadcasted_iota(jnp.int32, (TC, C), 0)
    for part in range(4):
        grad = dot_rows(mg_ref[part * 160 : (part + 1) * 160, :], point_ref[...])
        sg_scr[1, 1 + 5 * part : 6 + 5 * part] = grad.astype(LOW).astype(F32).reshape(5, TC, C)
    for shift in range(3):
        for row in (0, TR + 1):
            sg_scr[shift, row] = jnp.zeros((TC, C), F32)

    def shift_and_taps(step, sums):
        for r in [STEP_ROWS * step + k for k in range(STEP_ROWS)]:
            sums = shift_row(r, sums)
        return sums

    def shift_row(r, sums):
        x = sg_scr[1, r + 1]
        sg_scr[0, r + 1] = jnp.where(col == TC - 1, 0.0, pltpu.roll(x, TC - 1, 0))
        sg_scr[2, r + 1] = jnp.where(col == 0, 0.0, pltpu.roll(x, 1, 0))
        return tuple(
            sums[k] + fold(x * wide_ref[k % 3, r + k // 3].astype(F32)) for k in range(9)
        )

    tap_sums = lax.fori_loop(
        0, TR // STEP_ROWS, shift_and_taps, tuple(jnp.zeros((8, C), F32) for _ in range(9))
    )

    def gradient(step, total):
        for r in [STEP_ROWS * step + k for k in range(STEP_ROWS)]:
            total = gradient_row(r, total)
        return total

    def gradient_row(r, total):
        acc = jnp.zeros((TC, C), F32)
        for row_off in range(3):
            for col_off in range(3):
                tap = taps_ref[row_off * 3 + col_off : row_off * 3 + col_off + 1, :]
                acc = acc + tap * sg_scr[col_off, r + 2 - row_off]
        acc = acc + jnp.where(col == 0, halo_scr[pl.ds(r, 1), :], 0.0)
        acc = acc + jnp.where(col == TC - 1, halo_scr[pl.ds(SIDE + r, 1), :], 0.0)
        rows = pl.ds(pl.multiple_of(r * TC, TC), TC)
        pre = ((mg_ref[rows, :].astype(F32) + acc) * slope_ref[rows, :]).astype(LOW)
        pre_ref[rows, :] = pre
        return total + fold(pre.astype(F32))

    bias_sum = lax.fori_loop(0, TR // STEP_ROWS, gradient, jnp.zeros((8, C), F32))

    tail = lax.broadcasted_iota(jnp.int32, (32, C), 0)
    total = jnp.zeros((32, C), F32)
    for f in range(4):
        total = jnp.where(tail == 4 * f + frame, jnp.sum(sums[f], axis=0, keepdims=True), total)
    for k in range(9):
        total = jnp.where(tail == 16 + k, jnp.sum(tap_sums[k], axis=0, keepdims=True), total)
    total = jnp.where(tail == 25, jnp.sum(bias_sum, axis=0, keepdims=True), total)

    small_ref[...] = total

    @pl.when(core == 0)
    def _():
        store_high(send_ref, rows_t_ref, spread_t_ref, pre_ref, mg_ref, small_ref)

    @pl.when(core != 0)
    def _():
        store_low(send_ref, rows_t_ref, pre_ref)


def put(ref, first, value):
    value = value.astype(ref.dtype)
    ref[first : first + value.shape[0], :] = value[:, :128]
    ref[HALF + first : HALF + first + value.shape[0], :] = value[:, 128:]


def store_low(ref, rows_t_ref, pre_ref):
    for first, count in ((0, 256), (256, 256), (512, 160)):
        put(ref, first, dot_plain(rows_t_ref[first : first + count, :], pre_ref[...]))


def store_high(ref, rows_t_ref, spread_t_ref, pre_ref, mg_ref, small_ref):
    for first, count in ((672, 160), (832, 192)):
        put(ref, first - HALF, dot_plain(rows_t_ref[first : first + count, :], pre_ref[...]))
    put(ref, 352, dot_plain(spread_t_ref[...], mg_ref[...]))
    put(ref, 608, small_ref[...])
    put(ref, 640, jnp.zeros((32, C), F32))


def keep_kernel(rows_t_ref, spread_t_ref, pre_ref, mg_ref, small_ref, keep_ref):
    core = lax.axis_index("core")

    @pl.when(core == 0)
    def _():
        store_low(keep_ref, rows_t_ref, pre_ref)

    @pl.when(core != 0)
    def _():
        store_high(keep_ref, rows_t_ref, spread_t_ref, pre_ref, mg_ref, small_ref)


def input_grad_kernel(pre_ref, w_ref, out_ref, wide_ref):
    step = PIXELS // 5
    for part in range(5):
        first = part * step
        for child in range(4):
            rows = dot_rows(pre_ref[first : first + step, :], w_ref[child * C : (child + 1) * C, :])
            for h in range(2):
                wide_ref[h, pl.ds(4 * first + child, step, stride=4), :] = rows[:, h * 128 : (h + 1) * 128]
    for h in range(2):
        out_ref[0, :, h * 128 : (h + 1) * 128] = wide_ref[h].astype(LOW)


def unpack_kernel(scale, low_ref, down_ref, bias_ref, taps_ref, point_ref, mix_ref):
    def take(first, count, side):
        start = first + side * HALF
        return low_ref[start : start + count, :].astype(F32) * scale

    for side in range(2):
        cols = slice(side * 128, side * 128 + 128)
        down_ref[0:HALF, cols] = take(0, HALF, side)
        down_ref[HALF:1024, cols] = take(2 * HALF, 352, side)
        point_ref[:, cols] = take(2 * HALF + 352, C, side)
        tail = take(2 * HALF + 608, 32, side)
        for f in range(4):
            mix_ref[f, :, cols] = tail[4 * f : 4 * f + 4, :]
        taps_ref[:, cols] = tail[16:25, :]
        bias_ref[:, cols] = tail[25:26, :]


def shape(dims, dtype):
    return jax.ShapeDtypeStruct(dims, dtype)


SMEM_SPEC = pl.BlockSpec(memory_space=pltpu.SMEM)
VMEM_SPEC = pl.BlockSpec(memory_space=pltpu.VMEM)


def call(kernel, name, specs, outs, scratch=()):
    return pl.pallas_call(
        kernel,
        name=name,
        in_specs=specs,
        out_specs=jax.tree.map(lambda _: VMEM_SPEC, outs),
        out_shape=outs,
        scratch_shapes=list(scratch),
        compiler_params=pltpu.CompilerParams(vmem_limit_bytes=VMEM_BYTES),
    )


def exchange_copies(chunk, axis):
    count = lax.axis_size(axis)
    wide = jnp.broadcast_to(chunk.astype(LOW)[None], (count,) + chunk.shape)
    return lax.all_to_all(wide, axis, split_axis=0, concat_axis=0, tiled=True)


def sum_over_devices(keep, send):
    got = lax.ppermute(send, "core", [(0, 1), (1, 0)])
    rows = (keep + got.astype(F32)).astype(LOW).reshape(lax.axis_size(("z", "x")), -1, 2, 128)
    got = lax.all_to_all(rows, ("z", "x"), split_axis=0, concat_axis=0, tiled=True)
    chunk = jnp.sum(got.astype(F32), axis=0)
    chunk = jnp.sum(exchange_copies(chunk, ("yl", "yh")).astype(F32), axis=0)
    rows = exchange_copies(chunk, ("z", "x")).reshape(2 * HALF, 128)
    return lax.all_gather(rows, "core", axis=0, tiled=True)


def on_device(
    activations, down_weight, down_bias, taps, point_weight, time_mix, edge_rows, cotangent
):
    frames = cotangent.shape[0]
    tiles = lax.axis_size(PIX)
    scale = 1.0 / math.sqrt(frames * tiles * PIXELS)
    swap = [(0, 1), (1, 0)]
    far_half = lax.ppermute(cotangent, "yh", swap)

    act_cols = activations.reshape(TR, 4 * TC, C)
    cot_cols = cotangent.reshape(frames, TR // frames, TC, C)
    even = lax.axis_index("yl") % 2 == 0
    west_act = act_cols[:, :4, :].reshape(4 * TR, C)
    east_act = act_cols[:, 4 * TC - 4 :, :].reshape(4 * TR, C)
    west_cot = cot_cols[:, :, 0, :].reshape(TR, C)
    east_cot = cot_cols[:, :, TC - 1, :].reshape(TR, C)

    def exchange(west, east, axes, hops):
        first = lax.ppermute(jnp.where(even, east, west), axes, hops(lambda i: i ^ 1))
        second = lax.ppermute(
            jnp.where(even, west, east), axes, hops(lambda i: (i + 2 * (i % 2) - 1) % tiles)
        )
        return jnp.where(even, second, first), jnp.where(even, first, second)

    from_west, from_east = exchange(
        jnp.concatenate([west_act, west_cot], axis=0),
        jnp.concatenate([east_act, east_cot], axis=0),
        PIX,
        lambda partner: [(i, partner(i)) for i in range(tiles)],
    )
    cross = exchange(
        west_cot,
        east_cot,
        ("yh",) + PIX,
        lambda partner: [
            (y * tiles + i, (1 - y) * tiles + partner(i)) for y in range(2) for i in range(tiles)
        ],
    )
    bias = down_bias.reshape(1, C)
    rows_t, pooled, slope = call(
        forward_kernel,
        "forward",
        [VMEM_SPEC] * 3,
        (shape((4 * C, PIXELS), LOW), shape((PIXELS, C), LOW), shape((PIXELS, C), F32)),
        [
            pltpu.VMEM((2, 4 * PIXELS, 128), F32),
        ],
    )(activations.reshape(4 * PIXELS, C), down_weight, bias)
    from_west, from_east, cross, pooled = lax.optimization_barrier(
        (from_west, from_east, cross, pooled)
    )
    edge_act = jnp.stack([from_west[: 4 * TR], from_east[: 4 * TR]])
    edge_pair = jnp.pad(
        jnp.stack([from_west[4 * TR :], from_east[4 * TR :], *cross]).reshape(
            4 * frames, TR // frames, C
        ),
        ((0, 0), (0, 3), (0, 0)),
    ).reshape(16 * 8, C)
    own = jnp.concatenate(
        [cotangent.reshape(PIXELS, C), far_half.reshape(PIXELS, C), edge_pair], axis=0
    )
    other = lax.ppermute(own, "core", swap)
    wide, spread_t, mixed = call(
        spread_kernel,
        "spread",
        [SMEM_SPEC] + [VMEM_SPEC] * 6,
        (shape((3, TR + 2, TC, C), LOW), shape((C, PIXELS), LOW), shape((PIXELS, C), LOW)),
        [
            pltpu.VMEM((2, 8 * SIDE, 128), F32),
            pltpu.VMEM((2 * SIDE, C), F32),
            pltpu.VMEM((3, TR + 2, TC, C), F32),
            pltpu.VMEM((PIXELS, C), LOW),
        ],
    )(edge_rows, edge_act, down_weight, bias, taps, point_weight, pooled)
    send, pre, mixed_grad, small = call(
        backward_kernel,
        "backward",
        [SMEM_SPEC] + [VMEM_SPEC] * 10,
        (
            shape((2 * HALF, 128), LOW),
            shape((PIXELS, C), LOW),
            shape((PIXELS, C), LOW),
            shape((32, C), F32),
        ),
        [
            pltpu.VMEM((3, TR + 2, TC, C), F32),
            pltpu.VMEM((96, C), F32),
            pltpu.VMEM((2 * SIDE, C), F32),
        ],
    )(edge_rows, own, other, time_mix, point_weight, taps, wide, spread_t, mixed, slope, rows_t)
    keep = call(keep_kernel, "keep", [VMEM_SPEC] * 5, shape((2 * HALF, 128), F32))(
        rows_t, spread_t, pre, mixed_grad, small
    )
    grad_input = call(
        input_grad_kernel,
        "input_grad",
        [VMEM_SPEC] * 2,
        shape((1, 4 * PIXELS, C), LOW),
        [pltpu.VMEM((2, 4 * PIXELS, 128), F32)],
    )(pre, down_weight)
    total = sum_over_devices(keep, send)
    grad_down, grad_bias, grad_taps, grad_point, grad_mix = call(
        functools.partial(unpack_kernel, scale),
        "unpack",
        [VMEM_SPEC],
        (
            shape((4 * C, C), F32),
            shape((1, C), F32),
            shape((9, C), F32),
            shape((C, C), F32),
            shape((frames, frames, C), F32),
        ),
    )(total)
    return grad_input, grad_down, grad_bias.reshape(C), grad_taps, grad_point, grad_mix


def solution(mesh):
    yl = mesh.shape["pix"] // 32 if mesh.shape["pix"] >= 128 else 2
    x, z = (4, 8) if mesh.shape["pix"] >= 128 else (2, 2)
    chips = Mesh(mesh.devices.reshape(2, 2, x, z, yl), ("yh", "core", "x", "z", "yl"))
    in_specs = (
        P(TM, PIX, None),
        P(),
        P(),
        P(),
        P(),
        P(),
        P(PIX, None, None),
        P(None, PIX + TM, None),
    )
    out_specs = (P(TM, PIX, None), P(), P(), P(), P(), P())
    return jax.shard_map(
        on_device, mesh=chips, in_specs=in_specs, out_specs=out_specs, check_vma=False
    )
```

```python
import functools
import math

import jax
import jax.numpy as jnp
from jax import lax
from jax.experimental import pallas as pl
from jax.experimental.pallas import tpu as pltpu
from jax.sharding import Mesh, PartitionSpec as P

C = 256
TR = 20
TC = 32
PIXELS = TR * TC
SIDE = 32
TM = ("yh", "core")
PIX = ("x", "z", "yl")
HALF = 672
STEP_ROWS = 4
LOW = jnp.bfloat16
F32 = jnp.float32
VMEM_BYTES = 24 << 20


def dot_plain(a, b):
    return jnp.dot(a, b, preferred_element_type=F32)


def dot_rows(a, b):
    return lax.dot_general(a, b, (((1,), (1,)), ((), ())), preferred_element_type=F32)


def every_fourth(ref, first, count):
    return jnp.concatenate([ref[h, pl.ds(first, count, stride=4), :] for h in range(2)], axis=1)


def forward_kernel(act_ref, w_ref, bias_ref, rows_t_ref, pooled_ref, slope_ref, wide_ref):
    step = PIXELS // 5
    for part in range(5):
        first = part * step
        span = slice(4 * first, 4 * first + 4 * step)
        for h in range(2):
            wide_ref[h, span, :] = act_ref[span, h * 128 : (h + 1) * 128].astype(F32)
        total = bias_ref[...]
        for child in range(4):
            rows = every_fourth(wide_ref, 4 * first + child, step).astype(LOW)
            total = total + dot_plain(rows, w_ref[child * C : (child + 1) * C, :])
            rows_t_ref[child * C : (child + 1) * C, first : first + step] = rows.T
        sigma = jax.nn.sigmoid(total)
        pooled_ref[first : first + step, :] = (total * sigma).astype(LOW)
        slope_ref[first : first + step, :] = sigma * (1.0 + total * (1.0 - sigma))


def own_kernel(cot_ref, far_ref, west_ref, east_ref, cross_west_ref, cross_east_ref, own_ref, pad_ref, sems):
    loads = [
        pltpu.make_async_copy(ref, own_ref.at[pl.ds(k * PIXELS, PIXELS), :], sems.at[k])
        for k, ref in enumerate((cot_ref, far_ref))
    ]
    for load in loads:
        load.start()
    pad_ref[...] = jnp.zeros_like(pad_ref)
    edges = ((west_ref, 4 * TR), (east_ref, 4 * TR), (cross_west_ref, 0), (cross_east_ref, 0))
    for k, (ref, first) in enumerate(edges):
        rows = ref[...].astype(F32)[first : first + TR]
        for f in range(4):
            place = 32 * k + 8 * f
            pad_ref[place : place + 5, :] = rows[5 * f : 5 * f + 5]
    own_ref[2 * PIXELS :, :] = pad_ref[...].astype(LOW)
    for load in loads:
        load.wait()


def flip_matrix(west_flip, east_flip, yh=None, core=None):
    row = lax.broadcasted_iota(jnp.int32, (2 * SIDE, 2 * SIDE), 0)
    col = lax.broadcasted_iota(jnp.int32, (2 * SIDE, 2 * SIDE), 1)
    east = row >= SIDE
    base = jnp.where(east, SIDE, 0)
    local = row - base
    flip = jnp.where(east, east_flip, west_flip)
    local = jnp.where(flip != 0, TR - 1 - local, local)
    if yh is not None:
        place = (local >= 10).astype(jnp.int32)
        rest = local - 10 * place
        other = (rest >= 5).astype(jnp.int32)
        local = jnp.where(place == yh, 0, 16) + jnp.where(other == core, 0, 8) + rest - 5 * other
    source = base + local
    return (col == source).astype(F32).astype(LOW)


def spread_kernel(
    maps_ref, edge_ref, w_ref, bias_ref, taps_ref, point_ref, pooled_ref,
    wide_low_ref, spread_t_ref, mixed_ref, edge_scr, halo_scr, wide_scr, spread_scr,
):
    edge_scr[...] = jnp.zeros_like(edge_scr)
    for side in range(2):
        for h in range(2):
            edge_scr[h, 4 * SIDE * side : 4 * SIDE * side + 4 * TR, :] = edge_ref[
                side, :, h * 128 : (h + 1) * 128
            ].astype(F32)
    total = bias_ref[...]
    for child in range(4):
        rows = every_fourth(edge_scr, child, 2 * SIDE).astype(LOW)
        total = total + dot_plain(rows, w_ref[child * C : (child + 1) * C, :])
    halo = (total * jax.nn.sigmoid(total)).astype(LOW)
    halo_scr[...] = dot_plain(flip_matrix(maps_ref[0, 0, 0], maps_ref[0, 1, 0]), halo)
    col = lax.broadcasted_iota(jnp.int32, (TC, C), 0)
    for shift in range(3):
        for row in (0, TR + 1):
            wide_scr[shift, row] = jnp.zeros((TC, C), F32)
            wide_low_ref[shift, row] = jnp.zeros((TC, C), LOW)

    def widen(step, carry):
        for r in [STEP_ROWS * step + k for k in range(STEP_ROWS)]:
            widen_row(r)
        return carry

    def widen_row(r):
        x = pooled_ref[pl.ds(pl.multiple_of(r * TC, TC), TC), :].astype(F32)
        left = jnp.where(col == 0, halo_scr[pl.ds(r, 1), :], pltpu.roll(x, 1, 0))
        right = jnp.where(col == TC - 1, halo_scr[pl.ds(SIDE + r, 1), :], pltpu.roll(x, TC - 1, 0))
        for shift, value in enumerate((left, x, right)):
            wide_scr[shift, r + 1] = value
            wide_low_ref[shift, r + 1] = value.astype(LOW)

    lax.fori_loop(0, TR // STEP_ROWS, widen, 0)

    def convolve(step, carry):
        for r in [STEP_ROWS * step + k for k in range(STEP_ROWS)]:
            convolve_row(r)
        return carry

    def convolve_row(r):
        acc = jnp.zeros((TC, C), F32)
        for row_off in range(3):
            for col_off in range(3):
                tap = taps_ref[row_off * 3 + col_off : row_off * 3 + col_off + 1, :]
                acc = acc + tap * wide_scr[col_off, r + row_off]
        spread_scr[pl.ds(pl.multiple_of(r * TC, TC), TC), :] = acc.astype(LOW)

    lax.fori_loop(0, TR // STEP_ROWS, convolve, 0)
    step = PIXELS // 5
    for part in range(5):
        span = slice(part * step, (part + 1) * step)
        rows = spread_scr[span, :]
        mixed_ref[span, :] = (pooled_ref[span, :].astype(F32) + dot_plain(rows, point_ref[...])).astype(LOW)
        spread_t_ref[:, span] = rows.T


def fold(x):
    return jnp.sum(x.reshape(x.shape[0] // 8, 8, C), axis=0)


def backward_kernel(
    maps_ref, own_ref, other_ref, mix_ref, point_ref, taps_ref, wide_ref, spread_t_ref,
    mixed_ref, slope_ref, rows_t_ref,
    send_ref, pre_ref, mg_ref, small_ref, sg_scr, edge_scr, halo_scr,
):
    yh = lax.axis_index("yh")
    core = lax.axis_index("core")
    frame = yh * 2 + core
    weights = [mix_ref[f, pl.ds(frame, 1), :] for f in range(4)]

    sums = tuple(jnp.zeros((8, C), F32) for _ in range(4))
    sources = [
        (ref, far, (yh if far == 0 else 1 - yh) * 320 + owner * 160)
        for ref, owner in ((own_ref, core), (other_ref, 1 - core))
        for far in range(2)
    ]

    def chunk(i, sums):
        start = pl.multiple_of(i * 32, 32)
        for ref, far, base in sources:
            at = pl.multiple_of(base + i * 32, 32)
            cots = [ref[pl.ds(far * 640 + f * 160 + start, 32), :].astype(F32) for f in range(4)]
            total = weights[0] * cots[0]
            for f in range(1, 4):
                total = total + weights[f] * cots[f]
            mg_ref[pl.ds(at, 32), :] = total.astype(LOW)
            mixed = mixed_ref[pl.ds(at, 32), :].astype(F32)
            sums = tuple(sums[f] + fold(mixed * cots[f]) for f in range(4))
        return sums

    sums = lax.fori_loop(0, 5, chunk, sums)

    halo_scr[...] = jnp.zeros_like(halo_scr)
    for index, ref in enumerate((own_ref, other_ref)):
        for far in range(2):
            for side in range(2):
                start = 1280 + far * 64 + side * 32
                group = ref[start : start + 32, :].astype(F32)
                total = weights[0] * group[0:5]
                for f in range(1, 4):
                    total = total + weights[f] * group[8 * f : 8 * f + 5]
                place = side * SIDE + far * 16 + index * 8
                halo_scr[place : place + 5, :] = total
    flipped = dot_plain(flip_matrix(maps_ref[0, 0, 0], maps_ref[0, 1, 0], yh, core), halo_scr[...].astype(LOW)).astype(LOW)
    edge_grad = dot_rows(flipped, point_ref[...]).astype(LOW).astype(F32)
    edge_scr[...] = jnp.zeros_like(edge_scr)
    valid = lax.broadcasted_iota(jnp.int32, (SIDE, C), 0) < TR
    for side in range(2):
        base = side * 48
        edge_scr[base + 8 : base + 8 + SIDE, :] = jnp.where(
            valid, edge_grad[side * SIDE : (side + 1) * SIDE, :], 0.0
        )
    for side in range(2):
        base = side * 48
        flip = maps_ref[0, side, 0] != 0
        total = jnp.zeros((24, C), F32)
        for row_off in range(3):
            plain = 3 * row_off + (2 if side == 0 else 0)
            turned = 3 * (2 - row_off) + (2 if side == 0 else 0)
            tap = jnp.where(flip, taps_ref[turned : turned + 1, :], taps_ref[plain : plain + 1, :])
            start = base + 9 - row_off
            total = total + tap * edge_scr[start : start + 24, :]
        halo_scr[side * SIDE : side * SIDE + 24, :] = total

    col = lax.broadcasted_iota(jnp.int32, (TC, C), 0)
    for part in range(4):
        grad = dot_rows(mg_ref[part * 160 : (part + 1) * 160, :], point_ref[...])
        sg_scr[1, 1 + 5 * part : 6 + 5 * part] = grad.astype(LOW).astype(F32).reshape(5, TC, C)
    for shift in range(3):
        for row in (0, TR + 1):
            sg_scr[shift, row] = jnp.zeros((TC, C), F32)

    def shift_and_taps(step, sums):
        for r in [STEP_ROWS * step + k for k in range(STEP_ROWS)]:
            sums = shift_row(r, sums)
        return sums

    def shift_row(r, sums):
        x = sg_scr[1, r + 1]
        sg_scr[0, r + 1] = jnp.where(col == TC - 1, 0.0, pltpu.roll(x, TC - 1, 0))
        sg_scr[2, r + 1] = jnp.where(col == 0, 0.0, pltpu.roll(x, 1, 0))
        return tuple(
            sums[k] + fold(x * wide_ref[k % 3, r + k // 3].astype(F32)) for k in range(9)
        )

    tap_sums = lax.fori_loop(
        0, TR // STEP_ROWS, shift_and_taps, tuple(jnp.zeros((8, C), F32) for _ in range(9))
    )

    def gradient(step, total):
        for r in [STEP_ROWS * step + k for k in range(STEP_ROWS)]:
            total = gradient_row(r, total)
        return total

    def gradient_row(r, total):
        acc = jnp.zeros((TC, C), F32)
        for row_off in range(3):
            for col_off in range(3):
                tap = taps_ref[row_off * 3 + col_off : row_off * 3 + col_off + 1, :]
                acc = acc + tap * sg_scr[col_off, r + 2 - row_off]
        acc = acc + jnp.where(col == 0, halo_scr[pl.ds(r, 1), :], 0.0)
        acc = acc + jnp.where(col == TC - 1, halo_scr[pl.ds(SIDE + r, 1), :], 0.0)
        rows = pl.ds(pl.multiple_of(r * TC, TC), TC)
        pre = ((mg_ref[rows, :].astype(F32) + acc) * slope_ref[rows, :]).astype(LOW)
        pre_ref[rows, :] = pre
        return total + fold(pre.astype(F32))

    bias_sum = lax.fori_loop(0, TR // STEP_ROWS, gradient, jnp.zeros((8, C), F32))

    tail = lax.broadcasted_iota(jnp.int32, (32, C), 0)
    total = jnp.zeros((32, C), F32)
    for f in range(4):
        total = jnp.where(tail == 4 * f + frame, jnp.sum(sums[f], axis=0, keepdims=True), total)
    for k in range(9):
        total = jnp.where(tail == 16 + k, jnp.sum(tap_sums[k], axis=0, keepdims=True), total)
    total = jnp.where(tail == 25, jnp.sum(bias_sum, axis=0, keepdims=True), total)

    small_ref[...] = total

    @pl.when(core == 0)
    def _():
        store_high(send_ref, rows_t_ref, spread_t_ref, pre_ref, mg_ref, small_ref)

    @pl.when(core != 0)
    def _():
        store_low(send_ref, rows_t_ref, pre_ref)


def put(ref, first, value):
    value = value.astype(ref.dtype)
    ref[first : first + value.shape[0], :] = value[:, :128]
    ref[HALF + first : HALF + first + value.shape[0], :] = value[:, 128:]


def store_low(ref, rows_t_ref, pre_ref):
    for first, count in ((0, 256), (256, 256), (512, 160)):
        put(ref, first, dot_plain(rows_t_ref[first : first + count, :], pre_ref[...]))


def store_high(ref, rows_t_ref, spread_t_ref, pre_ref, mg_ref, small_ref):
    for first, count in ((672, 160), (832, 192)):
        put(ref, first - HALF, dot_plain(rows_t_ref[first : first + count, :], pre_ref[...]))
    put(ref, 352, dot_plain(spread_t_ref[...], mg_ref[...]))
    put(ref, 608, small_ref[...])
    put(ref, 640, jnp.zeros((32, C), F32))


def keep_kernel(rows_t_ref, spread_t_ref, pre_ref, mg_ref, small_ref, keep_ref):
    core = lax.axis_index("core")

    @pl.when(core == 0)
    def _():
        store_low(keep_ref, rows_t_ref, pre_ref)

    @pl.when(core != 0)
    def _():
        store_high(keep_ref, rows_t_ref, spread_t_ref, pre_ref, mg_ref, small_ref)


def input_grad_kernel(pre_ref, w_ref, out_ref, wide_ref):
    step = PIXELS // 5
    for part in range(5):
        first = part * step
        for child in range(4):
            rows = dot_rows(pre_ref[first : first + step, :], w_ref[child * C : (child + 1) * C, :])
            for h in range(2):
                wide_ref[h, pl.ds(4 * first + child, step, stride=4), :] = rows[:, h * 128 : (h + 1) * 128]
    for h in range(2):
        out_ref[0, :, h * 128 : (h + 1) * 128] = wide_ref[h].astype(LOW)


def unpack_kernel(scale, low_ref, down_ref, bias_ref, taps_ref, point_ref, mix_ref):
    def take(first, count, side):
        start = first + side * HALF
        return low_ref[start : start + count, :].astype(F32) * scale

    for side in range(2):
        cols = slice(side * 128, side * 128 + 128)
        down_ref[0:HALF, cols] = take(0, HALF, side)
        down_ref[HALF:1024, cols] = take(2 * HALF, 352, side)
        point_ref[:, cols] = take(2 * HALF + 352, C, side)
        tail = take(2 * HALF + 608, 32, side)
        for f in range(4):
            mix_ref[f, :, cols] = tail[4 * f : 4 * f + 4, :]
        taps_ref[:, cols] = tail[16:25, :]
        bias_ref[:, cols] = tail[25:26, :]


def shape(dims, dtype):
    return jax.ShapeDtypeStruct(dims, dtype)


SMEM_SPEC = pl.BlockSpec(memory_space=pltpu.SMEM)
ANY_SPEC = pl.BlockSpec(memory_space=pl.ANY)
VMEM_SPEC = pl.BlockSpec(memory_space=pltpu.VMEM)


def call(kernel, name, specs, outs, scratch=()):
    return pl.pallas_call(
        kernel,
        name=name,
        in_specs=specs,
        out_specs=jax.tree.map(lambda _: VMEM_SPEC, outs),
        out_shape=outs,
        scratch_shapes=list(scratch),
        compiler_params=pltpu.CompilerParams(vmem_limit_bytes=VMEM_BYTES),
    )


def exchange_copies(chunk, axis):
    count = lax.axis_size(axis)
    wide = jnp.broadcast_to(chunk.astype(LOW)[None], (count,) + chunk.shape)
    return lax.all_to_all(wide, axis, split_axis=0, concat_axis=0, tiled=True)


def sum_over_devices(keep, send):
    got = lax.ppermute(send, "core", [(0, 1), (1, 0)])
    rows = (keep + got.astype(F32)).astype(LOW).reshape(lax.axis_size(("z", "x")), -1, 2, 128)
    got = lax.all_to_all(rows, ("z", "x"), split_axis=0, concat_axis=0, tiled=True)
    chunk = jnp.sum(got.astype(F32), axis=0)
    chunk = jnp.sum(exchange_copies(chunk, ("yl", "yh")).astype(F32), axis=0)
    rows = exchange_copies(chunk, ("z", "x")).reshape(2 * HALF, 128)
    return lax.all_gather(rows, "core", axis=0, tiled=True)


def on_device(
    activations, down_weight, down_bias, taps, point_weight, time_mix, edge_rows, cotangent
):
    frames = cotangent.shape[0]
    tiles = lax.axis_size(PIX)
    scale = 1.0 / math.sqrt(frames * tiles * PIXELS)
    swap = [(0, 1), (1, 0)]
    far_half = lax.ppermute(cotangent, "yh", swap)

    act_cols = activations.reshape(TR, 4 * TC, C)
    cot_cols = cotangent.reshape(frames, TR // frames, TC, C)
    even = lax.axis_index("yl") % 2 == 0
    west_act = act_cols[:, :4, :].reshape(4 * TR, C)
    east_act = act_cols[:, 4 * TC - 4 :, :].reshape(4 * TR, C)
    west_cot = cot_cols[:, :, 0, :].reshape(TR, C)
    east_cot = cot_cols[:, :, TC - 1, :].reshape(TR, C)

    def exchange(west, east, axes, hops):
        first = lax.ppermute(jnp.where(even, east, west), axes, hops(lambda i: i ^ 1))
        second = lax.ppermute(
            jnp.where(even, west, east), axes, hops(lambda i: (i + 2 * (i % 2) - 1) % tiles)
        )
        return jnp.where(even, second, first), jnp.where(even, first, second)

    from_west, from_east = exchange(
        jnp.concatenate([west_act, west_cot], axis=0),
        jnp.concatenate([east_act, east_cot], axis=0),
        PIX,
        lambda partner: [(i, partner(i)) for i in range(tiles)],
    )
    cross = exchange(
        west_cot,
        east_cot,
        ("yh",) + PIX,
        lambda partner: [
            (y * tiles + i, (1 - y) * tiles + partner(i)) for y in range(2) for i in range(tiles)
        ],
    )
    bias = down_bias.reshape(1, C)
    rows_t, pooled, slope = call(
        forward_kernel,
        "forward",
        [VMEM_SPEC] * 3,
        (shape((4 * C, PIXELS), LOW), shape((PIXELS, C), LOW), shape((PIXELS, C), F32)),
        [
            pltpu.VMEM((2, 4 * PIXELS, 128), F32),
        ],
    )(activations.reshape(4 * PIXELS, C), down_weight, bias)
    from_west, from_east, cross, pooled = lax.optimization_barrier(
        (from_west, from_east, cross, pooled)
    )
    edge_act = jnp.stack([from_west[: 4 * TR], from_east[: 4 * TR]])
    own = call(
        own_kernel,
        "own",
        [ANY_SPEC] * 2 + [VMEM_SPEC] * 4,
        shape((2 * PIXELS + 128, C), LOW),
        [pltpu.VMEM((128, C), F32), pltpu.SemaphoreType.DMA((2,))],
    )(cotangent.reshape(PIXELS, C), far_half.reshape(PIXELS, C), from_west, from_east, *cross)
    other = lax.ppermute(own, "core", swap)
    wide, spread_t, mixed = call(
        spread_kernel,
        "spread",
        [SMEM_SPEC] + [VMEM_SPEC] * 6,
        (shape((3, TR + 2, TC, C), LOW), shape((C, PIXELS), LOW), shape((PIXELS, C), LOW)),
        [
            pltpu.VMEM((2, 8 * SIDE, 128), F32),
            pltpu.VMEM((2 * SIDE, C), F32),
            pltpu.VMEM((3, TR + 2, TC, C), F32),
            pltpu.VMEM((PIXELS, C), LOW),
        ],
    )(edge_rows, edge_act, down_weight, bias, taps, point_weight, pooled)
    send, pre, mixed_grad, small = call(
        backward_kernel,
        "backward",
        [SMEM_SPEC] + [VMEM_SPEC] * 10,
        (
            shape((2 * HALF, 128), LOW),
            shape((PIXELS, C), LOW),
            shape((PIXELS, C), LOW),
            shape((32, C), F32),
        ),
        [
            pltpu.VMEM((3, TR + 2, TC, C), F32),
            pltpu.VMEM((96, C), F32),
            pltpu.VMEM((2 * SIDE, C), F32),
        ],
    )(edge_rows, own, other, time_mix, point_weight, taps, wide, spread_t, mixed, slope, rows_t)
    keep = call(keep_kernel, "keep", [VMEM_SPEC] * 5, shape((2 * HALF, 128), F32))(
        rows_t, spread_t, pre, mixed_grad, small
    )
    grad_input = call(
        input_grad_kernel,
        "input_grad",
        [VMEM_SPEC] * 2,
        shape((1, 4 * PIXELS, C), LOW),
        [pltpu.VMEM((2, 4 * PIXELS, 128), F32)],
    )(pre, down_weight)
    total = sum_over_devices(keep, send)
    grad_down, grad_bias, grad_taps, grad_point, grad_mix = call(
        functools.partial(unpack_kernel, scale),
        "unpack",
        [VMEM_SPEC],
        (
            shape((4 * C, C), F32),
            shape((1, C), F32),
            shape((9, C), F32),
            shape((C, C), F32),
            shape((frames, frames, C), F32),
        ),
    )(total)
    return grad_input, grad_down, grad_bias.reshape(C), grad_taps, grad_point, grad_mix


def solution(mesh):
    yl = mesh.shape["pix"] // 32 if mesh.shape["pix"] >= 128 else 2
    x, z = (4, 8) if mesh.shape["pix"] >= 128 else (2, 2)
    chips = Mesh(mesh.devices.reshape(2, 2, x, z, yl), ("yh", "core", "x", "z", "yl"))
    in_specs = (
        P(TM, PIX, None),
        P(),
        P(),
        P(),
        P(),
        P(),
        P(PIX, None, None),
        P(None, PIX + TM, None),
    )
    out_specs = (P(TM, PIX, None), P(), P(), P(), P(), P())
    return jax.shard_map(
        on_device, mesh=chips, in_specs=in_specs, out_specs=out_specs, check_vma=False
    )
```

```python
import functools
import math

import jax
import jax.numpy as jnp
from jax import lax
from jax.experimental import pallas as pl
from jax.experimental.pallas import tpu as pltpu
from jax.sharding import Mesh, PartitionSpec as P

C = 256
TR = 20
TC = 32
PIXELS = TR * TC
SIDE = 32
TM = ("yh", "core")
PIX = ("x", "z", "yl")
HALF = 672
STEP_ROWS = 4
LOW = jnp.bfloat16
F32 = jnp.float32
VMEM_BYTES = 24 << 20


def dot_plain(a, b):
    return jnp.dot(a, b, preferred_element_type=F32)


def dot_rows(a, b):
    return lax.dot_general(a, b, (((1,), (1,)), ((), ())), preferred_element_type=F32)


def every_fourth(ref, first, count):
    return jnp.concatenate([ref[h, pl.ds(first, count, stride=4), :] for h in range(2)], axis=1)


def forward_kernel(act_ref, w_ref, bias_ref, rows_t_ref, pooled_ref, slope_ref, wide_ref):
    step = PIXELS // 5
    for part in range(5):
        first = part * step
        span = slice(4 * first, 4 * first + 4 * step)
        for h in range(2):
            wide_ref[h, span, :] = act_ref[span, h * 128 : (h + 1) * 128].astype(F32)
        total = bias_ref[...]
        for child in range(4):
            rows = every_fourth(wide_ref, 4 * first + child, step).astype(LOW)
            total = total + dot_plain(rows, w_ref[child * C : (child + 1) * C, :])
            rows_t_ref[child * C : (child + 1) * C, first : first + step] = rows.T
        sigma = jax.nn.sigmoid(total)
        pooled_ref[first : first + step, :] = (total * sigma).astype(LOW)
        slope_ref[first : first + step, :] = sigma * (1.0 + total * (1.0 - sigma))


def own_kernel(cot_ref, far_ref, west_ref, east_ref, cross_west_ref, cross_east_ref, own_ref, pad_ref, sems):
    loads = [
        pltpu.make_async_copy(ref, own_ref.at[pl.ds(k * PIXELS, PIXELS), :], sems.at[k])
        for k, ref in enumerate((cot_ref, far_ref))
    ]
    for load in loads:
        load.start()
    pad_ref[...] = jnp.zeros_like(pad_ref)
    edges = ((west_ref, 4 * TR), (east_ref, 4 * TR), (cross_west_ref, 0), (cross_east_ref, 0))
    for k, (ref, first) in enumerate(edges):
        rows = ref[...].astype(F32)[first : first + TR]
        for f in range(4):
            place = 32 * k + 8 * f
            pad_ref[place : place + 5, :] = rows[5 * f : 5 * f + 5]
    own_ref[2 * PIXELS :, :] = pad_ref[...].astype(LOW)
    for load in loads:
        load.wait()


def flip_matrix(west_flip, east_flip, yh=None, core=None):
    row = lax.broadcasted_iota(jnp.int32, (2 * SIDE, 2 * SIDE), 0)
    col = lax.broadcasted_iota(jnp.int32, (2 * SIDE, 2 * SIDE), 1)
    east = row >= SIDE
    base = jnp.where(east, SIDE, 0)
    local = row - base
    flip = jnp.where(east, east_flip, west_flip)
    local = jnp.where(flip != 0, TR - 1 - local, local)
    if yh is not None:
        place = (local >= 10).astype(jnp.int32)
        rest = local - 10 * place
        other = (rest >= 5).astype(jnp.int32)
        local = jnp.where(place == yh, 0, 16) + jnp.where(other == core, 0, 8) + rest - 5 * other
    source = base + local
    return (col == source).astype(F32).astype(LOW)


def spread_kernel(
    maps_ref, edge_ref, w_ref, bias_ref, taps_ref, point_ref, pooled_ref,
    wide_low_ref, spread_t_ref, mixed_ref, edge_scr, halo_scr, wide_scr, spread_scr,
):
    edge_scr[...] = jnp.zeros_like(edge_scr)
    for side in range(2):
        for h in range(2):
            edge_scr[h, 4 * SIDE * side : 4 * SIDE * side + 4 * TR, :] = edge_ref[
                side, :, h * 128 : (h + 1) * 128
            ].astype(F32)
    total = bias_ref[...]
    for child in range(4):
        rows = every_fourth(edge_scr, child, 2 * SIDE).astype(LOW)
        total = total + dot_plain(rows, w_ref[child * C : (child + 1) * C, :])
    halo = (total * jax.nn.sigmoid(total)).astype(LOW)
    halo_scr[...] = dot_plain(flip_matrix(maps_ref[0, 0, 0], maps_ref[0, 1, 0]), halo)
    col = lax.broadcasted_iota(jnp.int32, (TC, C), 0)
    for shift in range(3):
        for row in (0, TR + 1):
            wide_scr[shift, row] = jnp.zeros((TC, C), F32)
            wide_low_ref[shift, row] = jnp.zeros((TC, C), LOW)

    def widen(step, carry):
        for r in [STEP_ROWS * step + k for k in range(STEP_ROWS)]:
            widen_row(r)
        return carry

    def widen_row(r):
        x = pooled_ref[pl.ds(pl.multiple_of(r * TC, TC), TC), :].astype(F32)
        left = jnp.where(col == 0, halo_scr[pl.ds(r, 1), :], pltpu.roll(x, 1, 0))
        right = jnp.where(col == TC - 1, halo_scr[pl.ds(SIDE + r, 1), :], pltpu.roll(x, TC - 1, 0))
        for shift, value in enumerate((left, x, right)):
            wide_scr[shift, r + 1] = value
            wide_low_ref[shift, r + 1] = value.astype(LOW)

    lax.fori_loop(0, TR // STEP_ROWS, widen, 0)

    def convolve(step, carry):
        for r in [STEP_ROWS * step + k for k in range(STEP_ROWS)]:
            convolve_row(r)
        return carry

    def convolve_row(r):
        acc = jnp.zeros((TC, C), F32)
        for row_off in range(3):
            for col_off in range(3):
                tap = taps_ref[row_off * 3 + col_off : row_off * 3 + col_off + 1, :]
                acc = acc + tap * wide_scr[col_off, r + row_off]
        spread_scr[pl.ds(pl.multiple_of(r * TC, TC), TC), :] = acc.astype(LOW)

    lax.fori_loop(0, TR // STEP_ROWS, convolve, 0)
    step = PIXELS // 5
    for part in range(5):
        span = slice(part * step, (part + 1) * step)
        rows = spread_scr[span, :]
        mixed_ref[span, :] = (pooled_ref[span, :].astype(F32) + dot_plain(rows, point_ref[...])).astype(LOW)
        spread_t_ref[:, span] = rows.T


def fold(x):
    return jnp.sum(x.reshape(x.shape[0] // 8, 8, C), axis=0)


def backward_kernel(
    maps_ref, own_ref, other_ref, mix_ref, point_ref, taps_ref, wide_ref, spread_t_ref,
    mixed_ref, slope_ref, rows_t_ref,
    send_ref, pre_ref, mg_ref, small_ref, sg_scr, edge_scr, halo_scr,
):
    yh = lax.axis_index("yh")
    core = lax.axis_index("core")
    frame = yh * 2 + core
    weights = [mix_ref[f, pl.ds(frame, 1), :] for f in range(4)]

    sums = tuple(jnp.zeros((8, C), F32) for _ in range(4))
    sources = [
        (ref, far, (yh if far == 0 else 1 - yh) * 320 + owner * 160)
        for ref, owner in ((own_ref, core), (other_ref, 1 - core))
        for far in range(2)
    ]

    def chunk(i, sums):
        start = pl.multiple_of(i * 32, 32)
        for ref, far, base in sources:
            at = pl.multiple_of(base + i * 32, 32)
            cots = [ref[pl.ds(far * 640 + f * 160 + start, 32), :].astype(F32) for f in range(4)]
            total = weights[0] * cots[0]
            for f in range(1, 4):
                total = total + weights[f] * cots[f]
            mg_ref[pl.ds(at, 32), :] = total.astype(LOW)
            mixed = mixed_ref[pl.ds(at, 32), :].astype(F32)
            sums = tuple(sums[f] + fold(mixed * cots[f]) for f in range(4))
        return sums

    sums = lax.fori_loop(0, 5, chunk, sums)

    halo_scr[...] = jnp.zeros_like(halo_scr)
    for index, ref in enumerate((own_ref, other_ref)):
        for far in range(2):
            for side in range(2):
                start = 1280 + far * 64 + side * 32
                group = ref[start : start + 32, :].astype(F32)
                total = weights[0] * group[0:5]
                for f in range(1, 4):
                    total = total + weights[f] * group[8 * f : 8 * f + 5]
                place = side * SIDE + far * 16 + index * 8
                halo_scr[place : place + 5, :] = total
    flipped = dot_plain(flip_matrix(maps_ref[0, 0, 0], maps_ref[0, 1, 0], yh, core), halo_scr[...].astype(LOW)).astype(LOW)
    edge_grad = dot_rows(flipped, point_ref[...]).astype(LOW).astype(F32)
    edge_scr[...] = jnp.zeros_like(edge_scr)
    valid = lax.broadcasted_iota(jnp.int32, (SIDE, C), 0) < TR
    for side in range(2):
        base = side * 48
        edge_scr[base + 8 : base + 8 + SIDE, :] = jnp.where(
            valid, edge_grad[side * SIDE : (side + 1) * SIDE, :], 0.0
        )
    for side in range(2):
        base = side * 48
        flip = maps_ref[0, side, 0] != 0
        total = jnp.zeros((24, C), F32)
        for row_off in range(3):
            plain = 3 * row_off + (2 if side == 0 else 0)
            turned = 3 * (2 - row_off) + (2 if side == 0 else 0)
            tap = jnp.where(flip, taps_ref[turned : turned + 1, :], taps_ref[plain : plain + 1, :])
            start = base + 9 - row_off
            total = total + tap * edge_scr[start : start + 24, :]
        halo_scr[side * SIDE : side * SIDE + 24, :] = total

    col = lax.broadcasted_iota(jnp.int32, (TC, C), 0)
    for part in range(4):
        grad = dot_rows(mg_ref[part * 160 : (part + 1) * 160, :], point_ref[...])
        sg_scr[1, 1 + 5 * part : 6 + 5 * part] = grad.astype(LOW).astype(F32).reshape(5, TC, C)
    for shift in range(3):
        for row in (0, TR + 1):
            sg_scr[shift, row] = jnp.zeros((TC, C), F32)

    def shift_and_taps(step, sums):
        for r in [STEP_ROWS * step + k for k in range(STEP_ROWS)]:
            sums = shift_row(r, sums)
        return sums

    def shift_row(r, sums):
        x = sg_scr[1, r + 1]
        sg_scr[0, r + 1] = jnp.where(col == TC - 1, 0.0, pltpu.roll(x, TC - 1, 0))
        sg_scr[2, r + 1] = jnp.where(col == 0, 0.0, pltpu.roll(x, 1, 0))
        return tuple(
            sums[k] + fold(x * wide_ref[k % 3, r + k // 3].astype(F32)) for k in range(9)
        )

    tap_sums = lax.fori_loop(
        0, TR // STEP_ROWS, shift_and_taps, tuple(jnp.zeros((8, C), F32) for _ in range(9))
    )

    def gradient(step, total):
        for r in [STEP_ROWS * step + k for k in range(STEP_ROWS)]:
            total = gradient_row(r, total)
        return total

    def gradient_row(r, total):
        acc = jnp.zeros((TC, C), F32)
        for row_off in range(3):
            for col_off in range(3):
                tap = taps_ref[row_off * 3 + col_off : row_off * 3 + col_off + 1, :]
                acc = acc + tap * sg_scr[col_off, r + 2 - row_off]
        acc = acc + jnp.where(col == 0, halo_scr[pl.ds(r, 1), :], 0.0)
        acc = acc + jnp.where(col == TC - 1, halo_scr[pl.ds(SIDE + r, 1), :], 0.0)
        rows = pl.ds(pl.multiple_of(r * TC, TC), TC)
        pre = ((mg_ref[rows, :].astype(F32) + acc) * slope_ref[rows, :]).astype(LOW)
        pre_ref[rows, :] = pre
        return total + fold(pre.astype(F32))

    bias_sum = lax.fori_loop(0, TR // STEP_ROWS, gradient, jnp.zeros((8, C), F32))

    tail = lax.broadcasted_iota(jnp.int32, (32, C), 0)
    total = jnp.zeros((32, C), F32)
    for f in range(4):
        total = jnp.where(tail == 4 * f + frame, jnp.sum(sums[f], axis=0, keepdims=True), total)
    for k in range(9):
        total = jnp.where(tail == 16 + k, jnp.sum(tap_sums[k], axis=0, keepdims=True), total)
    total = jnp.where(tail == 25, jnp.sum(bias_sum, axis=0, keepdims=True), total)

    small_ref[...] = total

    @pl.when(core == 0)
    def _():
        store_high(send_ref, rows_t_ref, spread_t_ref, pre_ref, mg_ref, small_ref)

    @pl.when(core != 0)
    def _():
        store_low(send_ref, rows_t_ref, pre_ref)


def put(ref, first, value):
    value = value.astype(ref.dtype)
    ref[first : first + value.shape[0], :] = value[:, :128]
    ref[HALF + first : HALF + first + value.shape[0], :] = value[:, 128:]


def store_low(ref, rows_t_ref, pre_ref):
    for first, count in ((0, 256), (256, 256), (512, 160)):
        put(ref, first, dot_plain(rows_t_ref[first : first + count, :], pre_ref[...]))


def store_high(ref, rows_t_ref, spread_t_ref, pre_ref, mg_ref, small_ref):
    for first, count in ((672, 160), (832, 192)):
        put(ref, first - HALF, dot_plain(rows_t_ref[first : first + count, :], pre_ref[...]))
    put(ref, 352, dot_plain(spread_t_ref[...], mg_ref[...]))
    put(ref, 608, small_ref[...])
    put(ref, 640, jnp.zeros((32, C), F32))


def keep_kernel(rows_t_ref, spread_t_ref, pre_ref, mg_ref, small_ref, keep_ref):
    core = lax.axis_index("core")

    @pl.when(core == 0)
    def _():
        store_low(keep_ref, rows_t_ref, pre_ref)

    @pl.when(core != 0)
    def _():
        store_high(keep_ref, rows_t_ref, spread_t_ref, pre_ref, mg_ref, small_ref)


def input_grad_kernel(pre_ref, w_ref, out_ref, wide_ref):
    step = PIXELS // 5
    for part in range(5):
        first = part * step
        for child in range(4):
            rows = dot_rows(pre_ref[first : first + step, :], w_ref[child * C : (child + 1) * C, :])
            for h in range(2):
                wide_ref[h, pl.ds(4 * first + child, step, stride=4), :] = rows[:, h * 128 : (h + 1) * 128]
    for h in range(2):
        out_ref[0, :, h * 128 : (h + 1) * 128] = wide_ref[h].astype(LOW)


def unpack_kernel(scale, low_ref, down_ref, bias_ref, taps_ref, point_ref, mix_ref):
    def take(first, count, side):
        start = first + side * HALF
        return low_ref[start : start + count, :].astype(F32) * scale

    for side in range(2):
        cols = slice(side * 128, side * 128 + 128)
        down_ref[0:HALF, cols] = take(0, HALF, side)
        down_ref[HALF:1024, cols] = take(2 * HALF, 352, side)
        point_ref[:, cols] = take(2 * HALF + 352, C, side)
        tail = take(2 * HALF + 608, 32, side)
        for f in range(4):
            mix_ref[f, :, cols] = tail[4 * f : 4 * f + 4, :]
        taps_ref[:, cols] = tail[16:25, :]
        bias_ref[:, cols] = tail[25:26, :]


def shape(dims, dtype):
    return jax.ShapeDtypeStruct(dims, dtype)


SMEM_SPEC = pl.BlockSpec(memory_space=pltpu.SMEM)
ANY_SPEC = pl.BlockSpec(memory_space=pl.ANY)
VMEM_SPEC = pl.BlockSpec(memory_space=pltpu.VMEM)


def call(kernel, name, specs, outs, scratch=()):
    return pl.pallas_call(
        kernel,
        name=name,
        in_specs=specs,
        out_specs=jax.tree.map(lambda _: VMEM_SPEC, outs),
        out_shape=outs,
        scratch_shapes=list(scratch),
        compiler_params=pltpu.CompilerParams(vmem_limit_bytes=VMEM_BYTES),
    )


def exchange_copies(chunk, axis):
    count = lax.axis_size(axis)
    wide = jnp.broadcast_to(chunk.astype(LOW)[None], (count,) + chunk.shape)
    return lax.all_to_all(wide, axis, split_axis=0, concat_axis=0, tiled=True)


def sum_over_devices(keep, send):
    got = lax.ppermute(send, "core", [(0, 1), (1, 0)])
    rows = (keep + got.astype(F32)).astype(LOW).reshape(lax.axis_size(("z", "x")), -1, 2, 128)
    got = lax.all_to_all(rows, ("z", "x"), split_axis=0, concat_axis=0, tiled=True)
    chunk = jnp.sum(got.astype(F32), axis=0)
    chunk = jnp.sum(exchange_copies(chunk, ("yl", "yh")).astype(F32), axis=0)
    rows = exchange_copies(chunk, ("z", "x")).reshape(2 * HALF, 128)
    return lax.all_gather(rows, "core", axis=0, tiled=True)


def on_device(
    activations, down_weight, down_bias, taps, point_weight, time_mix, edge_rows, cotangent
):
    frames = cotangent.shape[0]
    tiles = lax.axis_size(PIX)
    scale = 1.0 / math.sqrt(frames * tiles * PIXELS)
    swap = [(0, 1), (1, 0)]
    far_half = lax.ppermute(cotangent, "yh", swap)

    act_cols = activations.reshape(TR, 4 * TC, C)
    cot_cols = cotangent.reshape(frames, TR // frames, TC, C)
    even = lax.axis_index("yl") % 2 == 0
    west_act = act_cols[:, :4, :].reshape(4 * TR, C)
    east_act = act_cols[:, 4 * TC - 4 :, :].reshape(4 * TR, C)
    west_cot = cot_cols[:, :, 0, :].reshape(TR, C)
    east_cot = cot_cols[:, :, TC - 1, :].reshape(TR, C)

    bias = down_bias.reshape(1, C)
    rows_t, pooled, slope = call(
        forward_kernel,
        "forward",
        [VMEM_SPEC] * 3,
        (shape((4 * C, PIXELS), LOW), shape((PIXELS, C), LOW), shape((PIXELS, C), F32)),
        [
            pltpu.VMEM((2, 4 * PIXELS, 128), F32),
        ],
    )(activations.reshape(4 * PIXELS, C), down_weight, bias)

    def exchange(west, east, axes, hops, after=None):
        near = jnp.where(even, east, west)
        if after is not None:
            near, _ = lax.optimization_barrier((near, after))
        first = lax.ppermute(near, axes, hops(lambda i: i ^ 1))
        second = lax.ppermute(
            jnp.where(even, west, east), axes, hops(lambda i: (i + 2 * (i % 2) - 1) % tiles)
        )
        return jnp.where(even, second, first), jnp.where(even, first, second)

    from_west, from_east = exchange(
        jnp.concatenate([west_act, west_cot], axis=0),
        jnp.concatenate([east_act, east_cot], axis=0),
        PIX,
        lambda partner: [(i, partner(i)) for i in range(tiles)],
        pooled,
    )
    cross = exchange(
        west_cot,
        east_cot,
        ("yh",) + PIX,
        lambda partner: [
            (y * tiles + i, (1 - y) * tiles + partner(i)) for y in range(2) for i in range(tiles)
        ],
    )
    from_west, from_east, cross, pooled = lax.optimization_barrier(
        (from_west, from_east, cross, pooled)
    )
    edge_act = jnp.stack([from_west[: 4 * TR], from_east[: 4 * TR]])
    own = call(
        own_kernel,
        "own",
        [ANY_SPEC] * 2 + [VMEM_SPEC] * 4,
        shape((2 * PIXELS + 128, C), LOW),
        [pltpu.VMEM((128, C), F32), pltpu.SemaphoreType.DMA((2,))],
    )(cotangent.reshape(PIXELS, C), far_half.reshape(PIXELS, C), from_west, from_east, *cross)
    other = lax.ppermute(own, "core", swap)
    wide, spread_t, mixed = call(
        spread_kernel,
        "spread",
        [SMEM_SPEC] + [VMEM_SPEC] * 6,
        (shape((3, TR + 2, TC, C), LOW), shape((C, PIXELS), LOW), shape((PIXELS, C), LOW)),
        [
            pltpu.VMEM((2, 8 * SIDE, 128), F32),
            pltpu.VMEM((2 * SIDE, C), F32),
            pltpu.VMEM((3, TR + 2, TC, C), F32),
            pltpu.VMEM((PIXELS, C), LOW),
        ],
    )(edge_rows, edge_act, down_weight, bias, taps, point_weight, pooled)
    send, pre, mixed_grad, small = call(
        backward_kernel,
        "backward",
        [SMEM_SPEC] + [VMEM_SPEC] * 10,
        (
            shape((2 * HALF, 128), LOW),
            shape((PIXELS, C), LOW),
            shape((PIXELS, C), LOW),
            shape((32, C), F32),
        ),
        [
            pltpu.VMEM((3, TR + 2, TC, C), F32),
            pltpu.VMEM((96, C), F32),
            pltpu.VMEM((2 * SIDE, C), F32),
        ],
    )(edge_rows, own, other, time_mix, point_weight, taps, wide, spread_t, mixed, slope, rows_t)
    keep = call(keep_kernel, "keep", [VMEM_SPEC] * 5, shape((2 * HALF, 128), F32))(
        rows_t, spread_t, pre, mixed_grad, small
    )
    grad_input = call(
        input_grad_kernel,
        "input_grad",
        [VMEM_SPEC] * 2,
        shape((1, 4 * PIXELS, C), LOW),
        [pltpu.VMEM((2, 4 * PIXELS, 128), F32)],
    )(pre, down_weight)
    total = sum_over_devices(keep, send)
    grad_down, grad_bias, grad_taps, grad_point, grad_mix = call(
        functools.partial(unpack_kernel, scale),
        "unpack",
        [VMEM_SPEC],
        (
            shape((4 * C, C), F32),
            shape((1, C), F32),
            shape((9, C), F32),
            shape((C, C), F32),
            shape((frames, frames, C), F32),
        ),
    )(total)
    return grad_input, grad_down, grad_bias.reshape(C), grad_taps, grad_point, grad_mix


def solution(mesh):
    yl = mesh.shape["pix"] // 32 if mesh.shape["pix"] >= 128 else 2
    x, z = (4, 8) if mesh.shape["pix"] >= 128 else (2, 2)
    chips = Mesh(mesh.devices.reshape(2, 2, x, z, yl), ("yh", "core", "x", "z", "yl"))
    in_specs = (
        P(TM, PIX, None),
        P(),
        P(),
        P(),
        P(),
        P(),
        P(PIX, None, None),
        P(None, PIX + TM, None),
    )
    out_specs = (P(TM, PIX, None), P(), P(), P(), P(), P())
    return jax.shard_map(
        on_device, mesh=chips, in_specs=in_specs, out_specs=out_specs, check_vma=False
    )
```
